32 devices in a mesh: section: 2 (over y), gy: 4 (over x, core), gx: 4 (over z).
Axes of the slice: x: 2, y: 2, z: 4, core: 2. Of those that a mesh axis runs over, the one named last changes fastest.
Arguments:
- streams: bfloat16 [2, 256, 256, 320], P('section', 'gy', 'gx'), may hold values from -24 to 24
- mask: int32 [256, 256], P('gy', 'gx'), may hold values 0 or 1
- timestep: int32 [1], replicated, may hold values from 0 to 999
- conv_weight: bfloat16 [2, 2, 3, 3, 320, 320], P('section'), may hold values from -0.109375 to 0.109375
- norm_gain: bfloat16 [2, 2, 320], P('section'), may hold values from 0.5 to 2
- time_weight: bfloat16 [2, 320, 320], P('section'), may hold values from -0.3125 to 0.3125
- cloud_vec: bfloat16 [2, 320], P('section'), may hold values from -4 to 4
- zero_weight: bfloat16 [320, 320], replicated, may hold values from -0.3125 to 0.3125
Outputs:
- conditioned: bfloat16 [256, 256, 320], P('gy', 'gx', 'section')
The draws below stay inside these ranges and needn't reach their ends.
All inputs are finite; a program needn't handle non-finite values. No bound on the sum of `mask` on one device may be relied on, other than what follows from the above.
Results may differ from the reference program's by a relative error of at most 0.0065.
Values may be sent and summed in bfloat16 or wider, within the bound.
A program may use at most 128 MiB of HBM per device.

```python
import math
import jax
import jax.numpy as jnp
from jax import lax

CHANNELS = 320
GROUPS = 32
HEIGHT = 256
WIDTH = 256


def draw_streams(key, part):
    key_base, key_pixel, key_chan = jax.random.split(key, 3)
    row_ramp = jnp.arange(HEIGHT, dtype=jnp.float32) / max(HEIGHT - 1, 1)
    col_ramp = jnp.arange(WIDTH, dtype=jnp.float32) / max(WIDTH - 1, 1)
    ramp = jnp.exp(jnp.log(3.0) * 0.5 * (row_ramp[:, None] + col_ramp[None, :]))
    pixel_scale = jnp.exp(jax.random.uniform(key_pixel, (2, HEIGHT, WIDTH), minval=0.0, maxval=jnp.log(3.4)))
    chan_scale = jnp.exp(jax.random.uniform(key_chan, (2, 1, 1, CHANNELS), minval=0.0, maxval=jnp.log(2.0)))
    base = jnp.clip(jax.random.normal(key_base, (2, HEIGHT, WIDTH, CHANNELS)), -4.0, 4.0)
    values = 0.3 * base * (ramp[None] * pixel_scale)[:, :, :, None] * chan_scale
    return values.astype(jnp.bfloat16)


def touch_ends(values, key, least, largest):
    longest = values.shape.index(max(values.shape))
    spots = []
    for shift in (0, 1):
        where = [jax.random.randint(jax.random.fold_in(key, axis), (), 0, length) for axis, length in enumerate(values.shape)]
        where[longest] = (where[longest] + shift) % values.shape[longest]
        spots.append(tuple(where))
    return values.at[spots[0]].set(least).at[spots[1]].set(largest)


def block_scale(rng, shape, pieces, low, high):
    loudness = 1.0
    for axis_at, shards_of in pieces:
        steps = jax.random.uniform(jax.random.fold_in(jax.random.fold_in(rng, 6), axis_at), (shards_of,), jnp.float32, low / len(pieces), high / len(pieces))
        loudness = loudness * jnp.repeat(jnp.exp(steps), shape[axis_at] // shards_of).reshape((-1,) + (1,) * (len(shape) - 1 - axis_at))
    return loudness


def gaussian(own_key, dims, scale, limit, shards=(), kind=jnp.bfloat16):
    factor_of = block_scale(own_key, dims, shards, -0.22, 0.18) if shards else 1.0
    result = jax.random.normal(own_key, dims, jnp.float32) * scale * factor_of
    return jnp.minimum(jnp.maximum(result, -limit), limit).astype(kind)


def setup_inputs(seed: int = 0) -> dict:
    streams_of = jax.random.split(jax.random.key(seed), 9)
    streams = draw_streams(jax.random.fold_in(streams_of[8], 71), 0)
    mask = touch_ends((jax.random.randint(streams_of[1], (HEIGHT, WIDTH), 0, 3) < 1).astype(jnp.int32), jax.random.fold_in(streams_of[1], 1), 0, 1)
    timestep = jax.random.randint(streams_of[2], (1,), 0, 1000).astype(jnp.int32)
    conv_weight = gaussian(streams_of[3], (2, 2, 3, 3, CHANNELS, CHANNELS), (9 * CHANNELS) ** -0.5, 0.109375, ((0, 2),))
    norm_gain = jnp.clip(jnp.exp(math.log(2.0) - 1.3862944 * jax.random.uniform(streams_of[4], (2, 2, CHANNELS), jnp.float32) ** block_scale(streams_of[4], (2, 2, CHANNELS), ((0, 2),), -0.2, 0.2)), 0.5, 2.0).astype(jnp.bfloat16)
    time_weight = gaussian(streams_of[5], (2, CHANNELS, CHANNELS), CHANNELS ** -0.5, 0.3125, ((0, 2),))
    cloud_vec = gaussian(streams_of[6], (2, CHANNELS), 1.0, 4.0, ((0, 2),))
    zero_weight = gaussian(streams_of[7], (CHANNELS, CHANNELS), CHANNELS ** -0.5, 0.3125)
    return dict(streams=streams, mask=mask, timestep=timestep, conv_weight=conv_weight, norm_gain=norm_gain, time_weight=time_weight, cloud_vec=cloud_vec, zero_weight=zero_weight)


def group_norm(field, gain):
    height, width, channels = field.shape
    grouped = field.reshape(height * width, GROUPS, channels // GROUPS)
    mean_value = lax.optimization_barrier(jnp.mean(grouped, axis=(0, 2)))
    centered = grouped - mean_value[None, :, None]
    spread = lax.optimization_barrier(jnp.mean(centered * centered, axis=(0, 2)))
    normed = centered * lax.rsqrt(spread + 1e-05)[None, :, None]
    return normed.reshape(height, width, channels) * gain

def conv_taps(field, weight):
    height, width, channels = field.shape
    padded = jnp.pad(field, ((1, 1), (1, 1), (0, 0)))
    summed = jnp.zeros((height * width, weight.shape[3]), jnp.float32)
    for tap_row in range(3):
        for tap_col in range(3):
            window = padded[tap_row:tap_row + height, tap_col:tap_col + width].reshape(height * width, channels)
            summed = summed + jnp.dot(window, weight[tap_row, tap_col], preferred_element_type=jnp.float32)
    return summed.reshape(height, width, weight.shape[3])

def reference(streams, mask, timestep, conv_weight, norm_gain, time_weight, cloud_vec, zero_weight):
    half_width = CHANNELS // 2
    freqs = jnp.exp(-math.log(10000.0) * jnp.arange(half_width, dtype=jnp.float32) / half_width)
    angles = timestep[0].astype(jnp.float32) * freqs
    sinus = jnp.concatenate([jnp.cos(angles), jnp.sin(angles)]).astype(jnp.bfloat16)
    flags = mask.astype(jnp.float32)[:, :, None]
    skips = []
    for stream in range(2):
        embedded = jax.nn.silu(jnp.dot(sinus[None], time_weight[stream], preferred_element_type=jnp.float32))[0]
        inputs = streams[stream].astype(jnp.float32) + flags * cloud_vec[stream].astype(jnp.float32)
        first = jax.nn.silu(group_norm(inputs, norm_gain[stream, 0].astype(jnp.float32))).astype(jnp.bfloat16)
        middle = conv_taps(first, conv_weight[stream, 0]) + embedded
        second = jax.nn.silu(group_norm(middle, norm_gain[stream, 1].astype(jnp.float32))).astype(jnp.bfloat16)
        skip = (inputs + conv_taps(second, conv_weight[stream, 1])).astype(jnp.bfloat16)
        skips.append(skip)
    residual = jnp.dot(skips[0].reshape(-1, CHANNELS), zero_weight, preferred_element_type=jnp.float32)
    residual = residual.reshape(HEIGHT, WIDTH, CHANNELS)
    return (skips[1].astype(jnp.float32) + residual).astype(jnp.bfloat16)
```

```python
import functools
import math

import jax
import jax.numpy as jnp
from jax import lax
from jax.experimental import pallas as pl
from jax.experimental.pallas import tpu as pltpu
from jax.sharding import PartitionSpec as P

GROUPS = 32
EPS = 1e-05
ROWS = 8
MAIN = 256
MESH = pl.DeviceIdType.MESH
VMEM = pltpu.VMEM


def bf16(*shape):
    return jax.ShapeDtypeStruct(shape, jnp.bfloat16)


def add_cloud(x, m, cloud_ref):
    channels = x.shape[1]
    m = jnp.concatenate([m] * pl.cdiv(channels, 128), axis=1)[:, :channels]
    return x + m * cloud_ref[...]


def load_inputs(x_ref, mask_ref, cloud_ref, start, count):
    x = x_ref[pl.ds(start, count), :].astype(jnp.float32)
    return add_cloud(x, mask_ref[pl.ds(start, count), :].astype(jnp.float32), cloud_ref)


def merge_stats(stat_ref, t, index):
    cells = t.shape[0]
    mean = jnp.sum(t, axis=0, keepdims=True) / cells
    diff = t - mean
    square = jnp.sum(diff * diff, axis=0, keepdims=True)
    k = jnp.asarray(index, jnp.float32)
    delta = mean - stat_ref[0:1, :]
    stat_ref[0:1, :] = stat_ref[0:1, :] + delta / (k + 1.0)
    stat_ref[1:2, :] = stat_ref[1:2, :] + square + delta * delta * (cells * k / (k + 1.0))


def store_columns(t, width, stage_ref, lane, index):
    count = t.shape[1]
    t3 = t.reshape(ROWS, width, count)
    at = pl.ds(pl.multiple_of(index * ROWS, ROWS), ROWS)
    stage_ref[0, at, lane:lane + count] = t3[:, 0, :]
    stage_ref[1, at, lane:lane + count] = t3[:, width - 1, :]


def split_rows(v):
    high = v.astype(jnp.bfloat16)
    left = v - high.astype(jnp.float32)
    mid = left.astype(jnp.bfloat16)
    low = (left - mid.astype(jnp.float32)).astype(jnp.bfloat16)
    return high, mid, low


def exact_dot(rows, matrix):
    count = rows.shape[0]
    parts = jnp.concatenate([p.astype(jnp.float32) for p in split_rows(rows)], axis=0).astype(jnp.bfloat16)
    y = jnp.dot(parts, matrix, preferred_element_type=jnp.float32)
    return y[0:count] + (y[count:2 * count] + y[2 * count:3 * count])


def group_matrices(channels):
    per = channels // GROUPS

    def member(shape, axis):
        c = lax.broadcasted_iota(jnp.int32, shape, axis)
        g = lax.broadcasted_iota(jnp.int32, shape, 1 - axis)
        return jnp.where((c >= g * per) & (c < g * per + per), 1.0, 0.0).astype(jnp.bfloat16)

    return member((channels, 128), 0), member((128, channels), 1)


def pack_stats(stat_ref, send_ref, cells, matrices):
    to_group, to_channel = matrices
    channels = stat_ref.shape[1]
    per = channels // GROUPS
    mean, square = stat_ref[0:1, :], stat_ref[1:2, :]
    total = exact_dot(jnp.broadcast_to(mean, (8, channels)), to_group)
    off = mean - exact_dot(total / per, to_channel)[0:1, :]
    square = square + cells * off * off
    squares = exact_dot(jnp.broadcast_to(square, (8, channels)), to_group)
    row = lax.broadcasted_iota(jnp.int32, (8, 128), 0)
    send_ref[...] = jnp.where(row < 1, total / per, squares)[0:2, :]


def group_factors(g_ref, gain, cells, matrices):
    n = g_ref.shape[0]
    per = gain.shape[1] // GROUPS
    values = g_ref[...]
    sums = jnp.sum(values, axis=0)
    mean = jnp.broadcast_to(sums[0:1, :] / n, (8, 128))
    off = values - mean[None, 0:2]
    total = sums[1:2, :] + float(cells * per) * jnp.sum(off * off, axis=0)[0:1, :]
    inverse = jnp.broadcast_to(lax.rsqrt(total / (float(cells) * n * per) + EPS), (8, 128))
    return exact_dot(mean, matrices[1])[0:1, :], exact_dot(inverse, matrices[1])[0:1, :] * gain


def kernel(ny, nx, height, width, mask_in, cloud_in, gain_in, sinus_in, x_hbm, time_hbm, zero_hbm, w_hbm, out_ref,
           x_ref, time_ref, zero_ref, main_ref, rest_ref, side_ref, embed_ref,
           mask_ref, mix_ref, cloud_ref, q_ref, mid_ref, keep_ref, out_buf, in_buf, stat_ref, stat_send, gathered,
           stage_ref, row_send, col_send, row_recv, col_recv, corner_recv, x_sem, w_sem, send, recv, swap_send, swap_recv):
    me_s, me_y, me_x = lax.axis_index("section"), lax.axis_index("gy"), lax.axis_index("gx")
    n = ny * nx
    channels = x_ref.shape[1]
    half = out_ref.shape[1]
    cells = ROWS * width
    chunks = height // ROWS
    other = {"section": 1 - me_s}

    def near(dy, dx):
        return {"gy": lax.rem(me_y + dy + ny, ny), "gx": lax.rem(me_x + dx + nx, nx)}

    def load_x(i):
        at = pl.ds(pl.multiple_of(i * cells, cells), cells)
        return pltpu.make_async_copy(x_hbm.at[at], x_ref.at[at], x_sem.at[i])

    for i in range(chunks):
        load_x(i).start()
    rest = channels - MAIN
    loads = []
    for k in range(2):
        loads.append([
            pltpu.make_async_copy(w_hbm.at[k, :, :, pl.ds(0, MAIN)], main_ref.at[k], w_sem.at[2 * k]),
            pltpu.make_async_copy(w_hbm.at[k, :, :, pl.ds(MAIN, rest)], rest_ref.at[k], w_sem.at[2 * k + 1]),
        ])
    small = [
        pltpu.make_async_copy(time_hbm, time_ref, w_sem.at[4]),
        pltpu.make_async_copy(zero_hbm, zero_ref, w_sem.at[5]),
    ]
    for copy in small + loads[0] + loads[1]:
        copy.start()
    barrier = pltpu.get_barrier_semaphore()
    for d in range(1, n):
        pl.semaphore_signal(barrier, inc=1, device_id=near(d // nx, d % nx), device_id_type=MESH)
    pl.semaphore_signal(barrier, inc=1, device_id=other, device_id_type=MESH)
    cloud_ref[...] = cloud_in[...].astype(jnp.float32)
    gains = gain_in[0].astype(jnp.float32)
    matrices = group_matrices(channels)
    load = functools.partial(load_inputs, x_ref, mask_ref, cloud_ref)

    valid_up, valid_down = me_y > 0, me_y < ny - 1
    valid_left, valid_right = me_x > 0, me_x < nx - 1
    early = height - 16

    def remote(src, dst, sends, receives, target):
        return pltpu.make_async_remote_copy(
            src_ref=src, dst_ref=dst, send_sem=sends, recv_sem=receives,
            device_id=target, device_id_type=MESH,
        )

    def edge_jobs(phase):
        lanes = pl.ds(0, 512 if phase == 0 else 384)
        first, last = pl.ds(0, 16), pl.ds(width - 16, 16)
        up, down = valid_up, valid_down
        left, right = valid_left, valid_right
        rows, corner = row_send.at[phase], corner_recv.at[phase]
        cols = col_send.at[phase]
        jobs = []
        for side, dy, to, back in ((0, -1, up, down), (1, 1, down, up)):
            base = 0 if side else 2
            jobs.append((("row", side), rows.at[side, :, lanes], row_recv.at[phase, 1 - side, :, lanes], (dy, 0), to, back))
            jobs.append((("row", side), rows.at[side, last, lanes], corner.at[base, :, lanes], (dy, 1), to & right, back & left))
            jobs.append((("row", side), rows.at[side, first, lanes], corner.at[base + 1, :, lanes], (dy, -1), to & left, back & right))
        for part, at in enumerate((pl.ds(0, early), pl.ds(early, 16))):
            jobs.append((("col", part), cols.at[1, at, lanes], col_recv.at[phase, 0, at, lanes], (0, 1), right, left))
            jobs.append((("col", part), cols.at[0, at, lanes], col_recv.at[phase, 1, at, lanes], (0, -1), left, right))
        return [
            (kind, functools.partial(remote, src, dst, send.at[phase, k], recv.at[phase, k], near(*step)), going, coming)
            for k, (kind, src, dst, step, going, coming) in enumerate(jobs)
        ]

    def start_edges(phase, *kinds):
        for kind, copy, going, _ in edge_jobs(phase):
            if kind in kinds:
                pl.when(going)(lambda: copy().start())

    def wait_edges(phase):
        for _, copy, going, coming in edge_jobs(phase):
            pl.when(going)(lambda: copy().wait_send())
            pl.when(coming)(lambda: copy().wait_recv())

    def pack_columns(phase, start, count):
        lanes = 512 if phase == 0 else 384
        for side in range(2):
            col_send[phase, side, start:start + count, 0:lanes] = stage_ref[side, start:start + count, 0:lanes].astype(jnp.bfloat16)

    def stat_copies(phase):
        order = sorted(range(1, n), key=lambda d: -min(d % nx, nx - d % nx))
        return [
            remote(stat_send.at[phase], gathered.at[phase, d], send.at[phase, 10 + d - 1], recv.at[phase, 10 + d - 1],
                   near(d // nx, d % nx))
            for d in order
        ]

    def exchange(phase):
        pack_stats(stat_ref, stat_send.at[phase], height * width, matrices)
        for copy in stat_copies(phase):
            copy.start()
        gathered[phase, 0] = stat_send[phase]
        for copy in loads[phase]:
            copy.wait()
        fill_sides(main_ref.at[phase], rest_ref.at[phase], side_ref)
        for copy in stat_copies(phase):
            copy.wait()
        factors = group_factors(gathered.at[phase], gains[phase:phase + 1], height * width, matrices)
        wait_edges(phase)
        return factors

    def filler(phase, source, mean, scale):
        half_scale = scale * 0.5

        def act(t, valid=None):
            z = (t - mean) * half_scale
            z = z + z * jnp.tanh(z)
            return z if valid is None else jnp.where(valid, z, 0.0)

        def border_act(v, valid):
            v = v.astype(jnp.float32)
            if phase == 0:
                t = add_cloud(v[:, :channels], v[:, 384:512], cloud_ref)
            else:
                t = v[:, :channels] + embed_ref[...]
            return act(t, valid)

        stage_ref[0, :, 0:channels] = border_act(col_recv[phase, 0], valid_left)
        stage_ref[1, :, 0:channels] = border_act(col_recv[phase, 1], valid_right)

        def chunk(i):
            at = pl.ds(pl.multiple_of(i * ROWS, ROWS), ROWS)
            fill_columns(
                q_ref, pl.multiple_of(i * cells + width, width),
                act(source(pl.multiple_of(i * cells, cells), cells)),
                stage_ref[0, at, 0:channels], stage_ref[1, at, 0:channels], ROWS, width,
            )

        def border(k, slot, valid):
            lcol = border_act(corner_recv[phase, 2 * k], valid_left & valid)[15:16, :]
            rcol = border_act(corner_recv[phase, 2 * k + 1], valid_right & valid)[0:1, :]
            fill_columns(
                q_ref, slot * width, border_act(row_recv[phase, k], valid), lcol, rcol, 1, width,
            )

        border(0, 0, valid_up)
        border(1, height + 1, valid_down)
        return chunk

    def run(chunk, step, after=None, late=None):
        chunk(0)
        begin = 0
        if after is not None:
            chunk(1)
            step(0)
            after()
            begin = 1

        def body(i, carry):
            chunk(i + 1)
            step(i)
            return carry

        lax.fori_loop(begin, chunks - 1, body, 0)
        if late is not None:
            late()
        step(chunks - 1)

    stat_ref[...] = jnp.zeros_like(stat_ref)
    ones = lax.broadcasted_iota(jnp.int32, (ROWS, ROWS * 128), 1) // 128
    ones = (ones == lax.broadcasted_iota(jnp.int32, (ROWS, ROWS * 128), 0)).astype(jnp.float32).astype(jnp.bfloat16)

    def spread_mask(i, carry):
        m = mask_in[pl.ds(pl.multiple_of(i * ROWS, ROWS), ROWS), :].astype(jnp.float32).astype(jnp.bfloat16)
        wide = lax.dot_general(m, ones, (((0,), (0,)), ((), ())), preferred_element_type=jnp.float32)
        for r in range(ROWS):
            at = pl.ds(pl.multiple_of(i * cells + r * width, width), width)
            mask_ref[at, :] = wide[:, r * 128:(r + 1) * 128].astype(jnp.bfloat16)
        return carry

    lax.fori_loop(0, chunks, spread_mask, 0)
    for copy in small:
        copy.wait()
    embed = jnp.broadcast_to(sinus_in[...].astype(jnp.float32), (16, channels)).astype(jnp.bfloat16)
    embed = jnp.dot(embed, time_ref[...], preferred_element_type=jnp.float32)[0:1, :]
    embed_ref[...] = embed / (1.0 + jnp.exp(-embed))
    zero = zero_ref[...].astype(jnp.float32)
    line = lax.broadcasted_iota(jnp.int32, (channels, 1), 0)

    def place(start, stop, count, repeat):
        lane = lax.broadcasted_iota(jnp.int32, (channels, count), 1)
        shift = (stop + half) % channels
        unit = jnp.where(line == lane + shift, 1.0, 0.0)
        part = jnp.where(me_s == 0, zero[:, stop:stop + count], unit).astype(jnp.float32)
        part = jnp.concatenate([part] * repeat, axis=1) if repeat > 1 else part
        mix_ref[:, start:start + count * repeat] = part.astype(jnp.bfloat16)

    mix_ref[:, 128:256] = jnp.zeros((channels, 128), jnp.bfloat16)
    place(0, 0, half, 1)
    place(256, half, 128, 1)
    place(384, half + 128, 32, 4)

    def first_stats(i, carry):
        load_x(i).wait()
        at = pl.ds(pl.multiple_of(i * cells, cells), cells)
        x, m = x_ref[at, :].astype(jnp.float32), mask_ref[at, :].astype(jnp.float32)
        store_columns(x, width, stage_ref, 0, i)
        store_columns(m, width, stage_ref, 384, i)
        merge_stats(stat_ref, add_cloud(x, m, cloud_ref), i)
        return carry

    lax.fori_loop(0, chunks, first_stats, 0)
    pack_columns(0, 0, height)
    for side, start in ((0, 0), (1, (height - 1) * width)):
        row_send[0, side, :, 0:channels] = x_ref[start:start + width, :]
        row_send[0, side, :, 384:512] = mask_ref[start:start + width, :]
    pl.semaphore_wait(barrier, n)
    start_edges(0, ("row", 0), ("row", 1), ("col", 0), ("col", 1))
    factors = exchange(0)
    stat_ref[...] = jnp.zeros_like(stat_ref)

    def first_step(i):
        t = conv_chunk(q_ref, main_ref.at[0], rest_ref.at[0], side_ref, i, width)
        store_columns(t, width, stage_ref, 0, i)
        t = t + embed_ref[...]
        mid_ref[pl.ds(pl.multiple_of(i * cells, cells), cells), :] = t
        merge_stats(stat_ref, t, i)

    def send_row(side, start):
        row_send[1, side, :, 0:channels] = (mid_ref[start:start + width, :] - embed_ref[...]).astype(jnp.bfloat16)
        start_edges(1, ("row", side))

    def send_early():
        pack_columns(1, 0, early)
        start_edges(1, ("col", 0))

    run(filler(0, load, *factors), first_step, lambda: send_row(0, 0), send_early)
    pack_columns(1, early, 16)
    start_edges(1, ("col", 1))
    send_row(1, (height - 1) * width)
    factors = exchange(1)
    quarter = cells // 4

    def swap(i):
        return pltpu.make_async_remote_copy(
            src_ref=out_buf.at[i], dst_ref=in_buf.at[i], send_sem=swap_send.at[i], recv_sem=swap_recv.at[i],
            device_id=other, device_id_type=MESH,
        )

    def second_step(i):
        at = pl.ds(pl.multiple_of(i * cells, cells), cells)
        t = load(pl.multiple_of(i * cells, cells), cells)
        skip = (t + conv_chunk(q_ref, main_ref.at[1], rest_ref.at[1], side_ref, i, width)).astype(jnp.bfloat16)
        y = jnp.dot(skip, mix_ref[...], preferred_element_type=jnp.float32)
        out_buf[i, 0:cells, :] = y[:, 256:384].astype(jnp.bfloat16)
        lane = lax.broadcasted_iota(jnp.int32, (quarter, 128), 1)
        rest = y[0:quarter, 384:512]
        for k in range(1, 4):
            rest = jnp.where(lane >= 32 * k, y[k * quarter:(k + 1) * quarter, 384:512], rest)
        out_buf[i, cells:cells + quarter, :] = rest.astype(jnp.bfloat16)
        swap(i).start()
        keep_ref[at, :] = y[:, :half]

    run(filler(1, lambda s, c: mid_ref[pl.ds(s, c), :], *factors), second_step)

    def finish(i, carry):
        swap(i).wait()
        rest = in_buf[i, cells:cells + quarter, :].astype(jnp.float32)
        for k in range(4):
            got = jnp.concatenate(
                [in_buf[i, k * quarter:(k + 1) * quarter, :].astype(jnp.float32), rest[:, 32 * k:32 * k + 32]], axis=1
            )
            at = pl.ds(pl.multiple_of(i * cells + k * quarter, quarter), quarter)
            out_ref[at, :] = (keep_ref[at, :] + got).astype(jnp.bfloat16)
        return carry

    lax.fori_loop(0, chunks, finish, 0)


def fill_columns(q_ref, start, act, lcol, rcol, rows, width):
    channels = act.shape[1]
    v = act.reshape(rows, width, channels)
    col = lax.broadcasted_iota(jnp.int32, v.shape, 1)
    vl = jnp.where(col == 0, lcol.reshape(rows, 1, channels), pltpu.roll(v, 1, 1))
    vr = jnp.where(col == width - 1, rcol.reshape(rows, 1, channels), pltpu.roll(v, width - 1, 1))
    at = pl.ds(start, rows * width)
    parts = [p.reshape(rows * width, channels) for p in (vl, v, vr)]
    for k, part in enumerate(parts):
        q_ref[at, k * MAIN:(k + 1) * MAIN] = part[:, :MAIN].astype(jnp.bfloat16)
    tails = [p[:, MAIN:] for p in parts]
    q_ref[at, 3 * MAIN:] = jnp.concatenate(tails, axis=1).astype(jnp.bfloat16)


def fill_sides(main_ref, rest_ref, side_ref):
    rest = side_ref.shape[2] // 4
    blank = jnp.zeros((3 * MAIN, rest), jnp.bfloat16)
    for r in range(6):
        top, low = [], []
        for k in range(4):
            dy = r - k
            inside = 0 <= dy <= 2
            top.append(main_ref[dy, :, :, MAIN:].reshape(3 * MAIN, rest) if inside else blank)
            low.append(rest_ref[dy, :, :, MAIN:].reshape(3 * rest, rest) if inside else blank[:3 * rest])
        side_ref[r, 0:3 * MAIN, :] = jnp.concatenate(top, axis=1)
        side_ref[r, 3 * MAIN:, :] = jnp.concatenate(low, axis=1)


def conv_chunk(q_ref, main_ref, rest_ref, side_ref, i, width):
    cells = ROWS * width
    rest = rest_ref.shape[2]

    def rows(start, count):
        return q_ref[pl.ds(pl.multiple_of((i * ROWS + start) * width, width), count * width), :]

    total = None
    for dy in range(3):
        w = jnp.concatenate(
            [main_ref[dy, :, :, 0:MAIN].reshape(3 * MAIN, MAIN), rest_ref[dy, :, :, 0:MAIN].reshape(3 * rest, MAIN)], axis=0
        )
        part = jnp.dot(rows(dy, ROWS), w, preferred_element_type=jnp.float32)
        total = part if total is None else total + part
    side = None
    for r in range(6):
        a = jnp.concatenate([rows(4 * k + r, 1) for k in range(ROWS // 4)], axis=0)
        part = jnp.dot(a, side_ref[r], preferred_element_type=jnp.float32)
        side = part if side is None else side + part
    side = jnp.concatenate(
        [side[k * width:(k + 1) * width, j * rest:(j + 1) * rest] for k in range(ROWS // 4) for j in range(4)], axis=0
    )
    return jnp.concatenate([total, side], axis=1)


def per_device(streams, mask, timestep, conv_weight, norm_gain, time_weight, cloud_vec, zero_weight):
    ny, nx = lax.axis_size("gy"), lax.axis_size("gx")
    height, width, channels = streams.shape[1:]
    cells = height * width
    half = channels // 2
    freqs = jnp.exp(-math.log(10000.0) * jnp.arange(half, dtype=jnp.float32) / half)
    angles = timestep[0].astype(jnp.float32) * freqs
    sinus = jnp.concatenate([jnp.cos(angles), jnp.sin(angles)]).astype(jnp.bfloat16)[None]
    x = streams.reshape(cells, channels)
    n = ny * nx
    rest = channels - MAIN
    chunks = height // ROWS
    piece = (chunks, ROWS * width * 5 // 4, 128)
    jobs = n - 1 + 10
    dma = pltpu.SemaphoreType.DMA
    vmem = pl.BlockSpec(memory_space=VMEM)
    hbm = pl.BlockSpec(memory_space=pl.ANY)
    f4, b2 = jnp.float32, jnp.bfloat16
    out = pl.pallas_call(
        functools.partial(kernel, ny, nx, height, width),
        out_shape=bf16(cells, half),
        in_specs=[vmem] * 4 + [hbm] * 4,
        out_specs=vmem,
        scratch_shapes=[
            VMEM((cells, channels), b2), VMEM((channels, channels), b2), VMEM((channels, channels), b2),
            VMEM((2, 3, 3, MAIN, channels), b2), VMEM((2, 3, 3, rest, channels), b2),
            VMEM((6, 3 * channels, 4 * rest), b2), VMEM((1, channels), f4),
            VMEM((cells, 128), b2), VMEM((channels, 512), b2),
            VMEM((1, channels), f4),
            VMEM(((height + 2) * width, 3 * channels), b2), VMEM((cells, channels), f4),
            VMEM((cells, half), f4), VMEM(piece, b2), VMEM(piece, b2),
            VMEM((8, channels), f4), VMEM((2, 2, 128), f4), VMEM((2, n, 2, 128), f4),
            VMEM((2, height, 512), f4),
            VMEM((2, 2, width, 512), b2), VMEM((2, 2, height, 512), b2),
            VMEM((2, 2, width, 512), b2), VMEM((2, 2, height, 512), b2), VMEM((2, 4, 16, 512), b2),
            dma((chunks,)), dma((6,)), dma((2, jobs)), dma((2, jobs)), dma((chunks,)), dma((chunks,)),
        ],
        compiler_params=pltpu.CompilerParams(
            collective_id=0, has_side_effects=True, vmem_limit_bytes=56 << 20
        ),
        name="block",
    )(mask, cloud_vec, norm_gain, sinus, x, time_weight[0], zero_weight, conv_weight[0])
    return out.reshape(height, width, half)


def solution(mesh):
    return jax.shard_map(
        per_device,
        mesh=mesh,
        in_specs=(
            P("section", "gy", "gx", None),
            P("gy", "gx"),
            P(),
            P("section", None, None, None, None, None),
            P("section", None, None),
            P("section", None, None),
            P("section", None),
            P(),
        ),
        out_specs=P("gy", "gx", "section"),
        check_vma=False,
    )
```

```python
import functools
import math

import jax
import jax.numpy as jnp
from jax import lax
from jax.experimental import pallas as pl
from jax.experimental.pallas import tpu as pltpu
from jax.sharding import PartitionSpec as P

GROUPS = 32
EPS = 1e-05
ROWS = 8
MAIN = 256
MESH = pl.DeviceIdType.MESH
VMEM = pltpu.VMEM


def bf16(*shape):
    return jax.ShapeDtypeStruct(shape, jnp.bfloat16)


def add_cloud(x, m, cloud_ref):
    channels = x.shape[1]
    m = jnp.concatenate([m] * pl.cdiv(channels, 128), axis=1)[:, :channels]
    return x + m * cloud_ref[...]


def load_inputs(x_ref, mask_ref, cloud_ref, start, count):
    x = x_ref[pl.ds(start, count), :].astype(jnp.float32)
    return add_cloud(x, mask_ref[pl.ds(start, count), :].astype(jnp.float32), cloud_ref)


def merge_stats(stat_ref, t, index):
    cells = t.shape[0]
    mean = jnp.sum(t, axis=0, keepdims=True) / cells
    diff = t - mean
    square = jnp.sum(diff * diff, axis=0, keepdims=True)
    k = jnp.asarray(index, jnp.float32)
    delta = mean - stat_ref[0:1, :]
    stat_ref[0:1, :] = stat_ref[0:1, :] + delta / (k + 1.0)
    stat_ref[1:2, :] = stat_ref[1:2, :] + square + delta * delta * (cells * k / (k + 1.0))


def store_columns(t, width, stage_ref, lane, index):
    count = t.shape[1]
    t3 = t.reshape(ROWS, width, count)
    at = pl.ds(pl.multiple_of(index * ROWS, ROWS), ROWS)
    stage_ref[0, at, lane:lane + count] = t3[:, 0, :]
    stage_ref[1, at, lane:lane + count] = t3[:, width - 1, :]


def split_rows(v):
    high = v.astype(jnp.bfloat16)
    left = v - high.astype(jnp.float32)
    mid = left.astype(jnp.bfloat16)
    low = (left - mid.astype(jnp.float32)).astype(jnp.bfloat16)
    return high, mid, low


def exact_dot(rows, matrix):
    count = rows.shape[0]
    parts = jnp.concatenate([p.astype(jnp.float32) for p in split_rows(rows)], axis=0).astype(jnp.bfloat16)
    y = jnp.dot(parts, matrix, preferred_element_type=jnp.float32)
    return y[0:count] + (y[count:2 * count] + y[2 * count:3 * count])


def group_matrices(channels):
    per = channels // GROUPS

    def member(shape, axis):
        c = lax.broadcasted_iota(jnp.int32, shape, axis)
        g = lax.broadcasted_iota(jnp.int32, shape, 1 - axis)
        return jnp.where((c >= g * per) & (c < g * per + per), 1.0, 0.0).astype(jnp.bfloat16)

    return member((channels, 128), 0), member((128, channels), 1)


def pack_stats(stat_ref, send_ref, cells, matrices):
    to_group, to_channel = matrices
    channels = stat_ref.shape[1]
    per = channels // GROUPS
    mean, square = stat_ref[0:1, :], stat_ref[1:2, :]
    total = exact_dot(jnp.broadcast_to(mean, (8, channels)), to_group)
    off = mean - exact_dot(total / per, to_channel)[0:1, :]
    square = square + cells * off * off
    squares = exact_dot(jnp.broadcast_to(square, (8, channels)), to_group)
    row = lax.broadcasted_iota(jnp.int32, (8, 128), 0)
    send_ref[...] = jnp.where(row < 1, total / per, squares)[0:2, :]


def group_factors(g_ref, gain, cells, matrices):
    n = g_ref.shape[0]
    per = gain.shape[1] // GROUPS
    values = g_ref[...]
    sums = jnp.sum(values, axis=0)
    mean = jnp.broadcast_to(sums[0:1, :] / n, (8, 128))
    off = values - mean[None, 0:2]
    total = sums[1:2, :] + float(cells * per) * jnp.sum(off * off, axis=0)[0:1, :]
    inverse = jnp.broadcast_to(lax.rsqrt(total / (float(cells) * n * per) + EPS), (8, 128))
    return exact_dot(mean, matrices[1])[0:1, :], exact_dot(inverse, matrices[1])[0:1, :] * gain


def kernel(ny, nx, height, width, step_in, mask_in, cloud_in, gain_in, x_hbm, time_hbm, zero_hbm, w_hbm, keep_hbm, got_hbm,
           x_ref, time_ref, zero_ref, main_ref, rest_ref, side_ref, embed_ref,
           mask_ref, mix_ref, cloud_ref, q_ref, mid_ref, keep_ref, out_buf, stat_ref, stat_send, gathered,
           stage_ref, row_send, col_send, row_recv, col_recv, corner_recv, x_sem, w_sem, send, recv, keep_sem, swap_send, swap_recv):
    me_s, me_y, me_x = lax.axis_index("section"), lax.axis_index("gy"), lax.axis_index("gx")
    n = ny * nx
    channels = x_ref.shape[1]
    half = keep_hbm.shape[1]
    cells = ROWS * width
    chunks = height // ROWS
    other = {"section": 1 - me_s}

    def near(dy, dx):
        return {"gy": lax.rem(me_y + dy + ny, ny), "gx": lax.rem(me_x + dx + nx, nx)}

    def load_x(i):
        at = pl.ds(pl.multiple_of(i * cells, cells), cells)
        return pltpu.make_async_copy(x_hbm.at[at], x_ref.at[at], x_sem.at[i])

    for i in range(chunks):
        load_x(i).start()
    rest = channels - MAIN
    loads = []
    for k in range(2):
        loads.append([
            pltpu.make_async_copy(w_hbm.at[k, :, :, pl.ds(0, MAIN)], main_ref.at[k], w_sem.at[2 * k]),
            pltpu.make_async_copy(w_hbm.at[k, :, :, pl.ds(MAIN, rest)], rest_ref.at[k], w_sem.at[2 * k + 1]),
        ])
    small = [
        pltpu.make_async_copy(time_hbm, time_ref, w_sem.at[4]),
        pltpu.make_async_copy(zero_hbm, zero_ref, w_sem.at[5]),
    ]
    for copy in small + loads[0] + loads[1]:
        copy.start()
    barrier = pltpu.get_barrier_semaphore()
    for d in range(1, n):
        pl.semaphore_signal(barrier, inc=1, device_id=near(d // nx, d % nx), device_id_type=MESH)
    pl.semaphore_signal(barrier, inc=1, device_id=other, device_id_type=MESH)
    cloud_ref[...] = cloud_in[...].astype(jnp.float32)
    gains = gain_in[0].astype(jnp.float32)
    matrices = group_matrices(channels)
    load = functools.partial(load_inputs, x_ref, mask_ref, cloud_ref)

    valid_up, valid_down = me_y > 0, me_y < ny - 1
    valid_left, valid_right = me_x > 0, me_x < nx - 1
    early = height - 16
    last_row = (height - 1) * width

    def remote(src, dst, sends, receives, target):
        return pltpu.make_async_remote_copy(
            src_ref=src, dst_ref=dst, send_sem=sends, recv_sem=receives,
            device_id=target, device_id_type=MESH,
        )

    def edge_jobs(phase):
        lanes = pl.ds(0, 512 if phase == 0 else 384)
        first, last = pl.ds(0, 16), pl.ds(width - 16, 16)
        up, down = valid_up, valid_down
        left, right = valid_left, valid_right
        rows, corner = row_send.at[phase], corner_recv.at[phase]
        cols = col_send.at[phase]
        jobs = []
        for side, dy, to, back in ((0, -1, up, down), (1, 1, down, up)):
            base = 0 if side else 2
            jobs.append((("row", side), rows.at[side, :, lanes], row_recv.at[phase, 1 - side, :, lanes], (dy, 0), to, back))
            jobs.append((("row", side), rows.at[side, last, lanes], corner.at[base, :, lanes], (dy, 1), to & right, back & left))
            jobs.append((("row", side), rows.at[side, first, lanes], corner.at[base + 1, :, lanes], (dy, -1), to & left, back & right))
        for part, at in enumerate((pl.ds(0, early), pl.ds(early, 16))):
            jobs.append((("col", part), cols.at[1, at, lanes], col_recv.at[phase, 0, at, lanes], (0, 1), right, left))
            jobs.append((("col", part), cols.at[0, at, lanes], col_recv.at[phase, 1, at, lanes], (0, -1), left, right))
        return [
            (kind, functools.partial(remote, src, dst, send.at[phase, k], recv.at[phase, k], near(*step)), going, coming)
            for k, (kind, src, dst, step, going, coming) in enumerate(jobs)
        ]

    def start_edges(phase, *kinds):
        for kind, copy, going, _ in edge_jobs(phase):
            if kind in kinds:
                pl.when(going)(lambda: copy().start())

    def wait_edges(phase):
        for _, copy, going, coming in edge_jobs(phase):
            pl.when(going)(lambda: copy().wait_send())
            pl.when(coming)(lambda: copy().wait_recv())

    def pack_columns(phase, start, count):
        lanes = 512 if phase == 0 else 384
        for side in range(2):
            col_send[phase, side, start:start + count, 0:lanes] = stage_ref[side, start:start + count, 0:lanes].astype(jnp.bfloat16)

    def stat_copies(phase):
        order = sorted(range(1, n), key=lambda d: -min(d % nx, nx - d % nx))
        return [
            remote(stat_send.at[phase], gathered.at[phase, d], send.at[phase, 10 + d - 1], recv.at[phase, 10 + d - 1],
                   near(d // nx, d % nx))
            for d in order
        ]

    def exchange(phase, send_edges):
        pack_stats(stat_ref, stat_send.at[phase], height * width, matrices)
        if phase == 0:
            pl.semaphore_wait(barrier, n)
        for copy in stat_copies(phase):
            copy.start()
        send_edges()
        gathered[phase, 0] = stat_send[phase]
        for copy in loads[phase]:
            copy.wait()
        fill_sides(main_ref.at[phase], rest_ref.at[phase], side_ref)
        for copy in stat_copies(phase):
            copy.wait()
        factors = group_factors(gathered.at[phase], gains[phase:phase + 1], height * width, matrices)
        wait_edges(phase)
        return factors

    def filler(phase, source, mean, scale):
        half_scale = scale * 0.5

        def act(t, valid=None):
            z = (t - mean) * half_scale
            z = z + z * jnp.tanh(z)
            return z if valid is None else jnp.where(valid, z, 0.0)

        def border_act(v, valid):
            v = v.astype(jnp.float32)
            if phase == 0:
                t = add_cloud(v[:, :channels], v[:, 384:512], cloud_ref)
            else:
                t = v[:, :channels] + embed_ref[...]
            return act(t, valid)

        stage_ref[0, :, 0:channels] = border_act(col_recv[phase, 0], valid_left)
        stage_ref[1, :, 0:channels] = border_act(col_recv[phase, 1], valid_right)

        def chunk(i):
            at = pl.ds(pl.multiple_of(i * ROWS, ROWS), ROWS)
            fill_columns(
                q_ref, pl.multiple_of(i * cells + width, width),
                act(source(pl.multiple_of(i * cells, cells), cells)),
                stage_ref[0, at, 0:channels], stage_ref[1, at, 0:channels], ROWS, width,
            )

        def border(k, slot, valid):
            lcol = border_act(corner_recv[phase, 2 * k], valid_left & valid)[15:16, :]
            rcol = border_act(corner_recv[phase, 2 * k + 1], valid_right & valid)[0:1, :]
            fill_columns(
                q_ref, slot * width, border_act(row_recv[phase, k], valid), lcol, rcol, 1, width,
            )

        border(0, 0, valid_up)
        border(1, height + 1, valid_down)
        return chunk

    def run(chunk, step, after=None, late=None):
        chunk(0)
        begin = 0
        if after is not None:
            chunk(1)
            step(0)
            after()
            begin = 1

        def body(i, carry):
            chunk(i + 1)
            step(i)
            return carry

        lax.fori_loop(begin, chunks - 1, body, 0)
        if late is not None:
            late()
        step(chunks - 1)

    stat_ref[...] = jnp.zeros_like(stat_ref)
    ones = lax.broadcasted_iota(jnp.int32, (ROWS, ROWS * 128), 1) // 128
    ones = (ones == lax.broadcasted_iota(jnp.int32, (ROWS, ROWS * 128), 0)).astype(jnp.float32).astype(jnp.bfloat16)

    def spread_mask(i, carry):
        m = mask_in[pl.ds(pl.multiple_of(i * ROWS, ROWS), ROWS), :].astype(jnp.float32).astype(jnp.bfloat16)
        wide = lax.dot_general(m, ones, (((0,), (0,)), ((), ())), preferred_element_type=jnp.float32)
        for r in range(ROWS):
            at = pl.ds(pl.multiple_of(i * cells + r * width, width), width)
            mask_ref[at, :] = wide[:, r * 128:(r + 1) * 128].astype(jnp.bfloat16)
        return carry

    lax.fori_loop(0, chunks, spread_mask, 0)
    for copy in small:
        copy.wait()
    angles = lax.broadcasted_iota(jnp.int32, (16, half), 1).astype(jnp.float32)
    angles = step_in[0].astype(jnp.float32) * jnp.exp(-math.log(10000.0) * angles / half)
    embed = sum(
        jnp.dot(wave(angles).astype(jnp.bfloat16), time_ref[k * half:(k + 1) * half, :], preferred_element_type=jnp.float32)
        for k, wave in enumerate((jnp.cos, jnp.sin))
    )[0:1, :]
    embed_ref[...] = embed / (1.0 + jnp.exp(-embed))
    zero = zero_ref[...].astype(jnp.float32)
    line = lax.broadcasted_iota(jnp.int32, (channels, 1), 0)

    def place(start, stop, count, repeat):
        lane = lax.broadcasted_iota(jnp.int32, (channels, count), 1)
        shift = (stop + half) % channels
        unit = jnp.where(line == lane + shift, 1.0, 0.0)
        part = jnp.where(me_s == 0, zero[:, stop:stop + count], unit).astype(jnp.float32)
        part = jnp.concatenate([part] * repeat, axis=1) if repeat > 1 else part
        mix_ref[:, start:start + count * repeat] = part.astype(jnp.bfloat16)

    mix_ref[:, 128:256] = jnp.zeros((channels, 128), jnp.bfloat16)
    place(0, 0, half, 1)
    place(256, half, 128, 1)
    place(384, half + 128, 32, 4)

    def first_stats(i, carry):
        load_x(i).wait()
        at = pl.ds(pl.multiple_of(i * cells, cells), cells)
        x, m = x_ref[at, :].astype(jnp.float32), mask_ref[at, :].astype(jnp.float32)
        store_columns(x, width, stage_ref, 0, i)
        store_columns(m, width, stage_ref, 384, i)
        merge_stats(stat_ref, add_cloud(x, m, cloud_ref), i)
        return carry

    lax.fori_loop(0, chunks, first_stats, 0)
    pack_columns(0, 0, height)
    for side, start in ((0, 0), (1, last_row)):
        row_send[0, side, :, 0:channels] = x_ref[start:start + width, :]
        row_send[0, side, :, 384:512] = mask_ref[start:start + width, :]
    factors = exchange(0, lambda: start_edges(0, ("row", 0), ("row", 1), ("col", 0), ("col", 1)))
    stat_ref[...] = jnp.zeros_like(stat_ref)

    def first_step(i):
        t = conv_chunk(q_ref, main_ref.at[0], rest_ref.at[0], side_ref, i, width)
        store_columns(t, width, stage_ref, 0, i)
        t = t + embed_ref[...]
        mid_ref[pl.ds(pl.multiple_of(i * cells, cells), cells), :] = t
        merge_stats(stat_ref, t, i)

    def send_row(side, start):
        row_send[1, side, :, 0:channels] = (mid_ref[start:start + width, :] - embed_ref[...]).astype(jnp.bfloat16)
        start_edges(1, ("row", side))

    def send_early():
        pack_columns(1, 0, early)
        start_edges(1, ("col", 0))

    run(filler(0, load, *factors), first_step, lambda: send_row(0, 0), send_early)

    def send_late():
        pack_columns(1, early, 16)
        start_edges(1, ("col", 1))
        send_row(1, last_row)

    factors = exchange(1, send_late)
    quarter = cells // 4

    def swap(i):
        return pltpu.make_async_remote_copy(
            src_ref=out_buf.at[i], dst_ref=got_hbm.at[i], send_sem=swap_send.at[i], recv_sem=swap_recv.at[i],
            device_id=other, device_id_type=MESH,
        )

    def store_keep(i):
        at = pl.ds(pl.multiple_of(i * cells, cells), cells)
        return pltpu.make_async_copy(keep_ref.at[at], keep_hbm.at[at], keep_sem.at[i])

    def second_step(i):
        at = pl.ds(pl.multiple_of(i * cells, cells), cells)
        t = load(pl.multiple_of(i * cells, cells), cells)
        skip = (t + conv_chunk(q_ref, main_ref.at[1], rest_ref.at[1], side_ref, i, width)).astype(jnp.bfloat16)
        y = jnp.dot(skip, mix_ref[...], preferred_element_type=jnp.float32)
        out_buf[i, 0:cells, :] = y[:, 256:384].astype(jnp.bfloat16)
        lane = lax.broadcasted_iota(jnp.int32, (quarter, 128), 1)
        rest = y[0:quarter, 384:512]
        for k in range(1, 4):
            rest = jnp.where(lane >= 32 * k, y[k * quarter:(k + 1) * quarter, 384:512], rest)
        out_buf[i, cells:cells + quarter, :] = rest.astype(jnp.bfloat16)
        swap(i).start()
        keep_ref[at, :] = y[:, :half].astype(jnp.bfloat16)
        store_keep(i).start()

    run(filler(1, lambda s, c: mid_ref[pl.ds(s, c), :], *factors), second_step)

    def finish(i, carry):
        store_keep(i).wait()
        swap(i).wait()
        return carry

    lax.fori_loop(0, chunks, finish, 0)


def merge_kernel(keep_ref, got_ref, out_hbm, out_ref, sem):
    chunks, cells = got_ref.shape[0], keep_ref.shape[0] // got_ref.shape[0]
    quarter = cells // 4

    def store(i):
        at = pl.ds(pl.multiple_of(i * cells, cells), cells)
        return pltpu.make_async_copy(out_ref.at[at], out_hbm.at[at], sem.at[i])

    def merge(i, carry):
        rest = got_ref[i, cells:, :].astype(jnp.float32)
        for k in range(4):
            got = got_ref[i, k * quarter:(k + 1) * quarter, :].astype(jnp.float32)
            got = jnp.concatenate([got, rest[:, 32 * k:32 * k + 32]], axis=1)
            at = pl.ds(pl.multiple_of(i * cells + k * quarter, quarter), quarter)
            out_ref[at, :] = (keep_ref[at, :].astype(jnp.float32) + got).astype(jnp.bfloat16)
        store(i).start()
        return carry

    lax.fori_loop(0, chunks, merge, 0)

    def finish(i, carry):
        store(i).wait()
        return carry

    lax.fori_loop(0, chunks, finish, 0)


def fill_columns(q_ref, start, act, lcol, rcol, rows, width):
    channels = act.shape[1]
    v = act.reshape(rows, width, channels)
    col = lax.broadcasted_iota(jnp.int32, v.shape, 1)
    vl = jnp.where(col == 0, lcol.reshape(rows, 1, channels), pltpu.roll(v, 1, 1))
    vr = jnp.where(col == width - 1, rcol.reshape(rows, 1, channels), pltpu.roll(v, width - 1, 1))
    at = pl.ds(start, rows * width)
    parts = [p.reshape(rows * width, channels) for p in (vl, v, vr)]
    for k, part in enumerate(parts):
        q_ref[at, k * MAIN:(k + 1) * MAIN] = part[:, :MAIN].astype(jnp.bfloat16)
    tails = [p[:, MAIN:] for p in parts]
    q_ref[at, 3 * MAIN:] = jnp.concatenate(tails, axis=1).astype(jnp.bfloat16)


def fill_sides(main_ref, rest_ref, side_ref):
    rest = side_ref.shape[2] // 4
    blank = jnp.zeros((3 * MAIN, rest), jnp.bfloat16)
    for r in range(6):
        top, low = [], []
        for k in range(4):
            dy = r - k
            inside = 0 <= dy <= 2
            top.append(main_ref[dy, :, :, MAIN:].reshape(3 * MAIN, rest) if inside else blank)
            low.append(rest_ref[dy, :, :, MAIN:].reshape(3 * rest, rest) if inside else blank[:3 * rest])
        side_ref[r, 0:3 * MAIN, :] = jnp.concatenate(top, axis=1)
        side_ref[r, 3 * MAIN:, :] = jnp.concatenate(low, axis=1)


def conv_chunk(q_ref, main_ref, rest_ref, side_ref, i, width):
    cells = ROWS * width
    rest = rest_ref.shape[2]

    def rows(start, count):
        return q_ref[pl.ds(pl.multiple_of((i * ROWS + start) * width, width), count * width), :]

    total = None
    for dy in range(3):
        w = jnp.concatenate(
            [main_ref[dy, :, :, 0:MAIN].reshape(3 * MAIN, MAIN), rest_ref[dy, :, :, 0:MAIN].reshape(3 * rest, MAIN)], axis=0
        )
        part = jnp.dot(rows(dy, ROWS), w, preferred_element_type=jnp.float32)
        total = part if total is None else total + part
    side = None
    for r in range(6):
        a = jnp.concatenate([rows(4 * k + r, 1) for k in range(ROWS // 4)], axis=0)
        part = jnp.dot(a, side_ref[r], preferred_element_type=jnp.float32)
        side = part if side is None else side + part
    side = jnp.concatenate(
        [side[k * width:(k + 1) * width, j * rest:(j + 1) * rest] for k in range(ROWS // 4) for j in range(4)], axis=0
    )
    return jnp.concatenate([total, side], axis=1)


def per_device(streams, mask, timestep, conv_weight, norm_gain, time_weight, cloud_vec, zero_weight):
    ny, nx = lax.axis_size("gy"), lax.axis_size("gx")
    height, width, channels = streams.shape[1:]
    cells = height * width
    half = channels // 2
    x = streams.reshape(cells, channels)
    n = ny * nx
    rest = channels - MAIN
    chunks = height // ROWS
    piece = (chunks, ROWS * width * 5 // 4, 128)
    jobs = n - 1 + 10
    dma = pltpu.SemaphoreType.DMA
    vmem = pl.BlockSpec(memory_space=VMEM)
    hbm = pl.BlockSpec(memory_space=pltpu.HBM)
    either = pl.BlockSpec(memory_space=pl.ANY)
    f4, b2 = jnp.float32, jnp.bfloat16
    keep, got = pl.pallas_call(
        functools.partial(kernel, ny, nx, height, width),
        out_shape=(VMEM((cells, half), b2), VMEM(piece, b2)),
        in_specs=[pl.BlockSpec(memory_space=pltpu.SMEM)] + [vmem] * 3 + [hbm] * 4,
        out_specs=(either, either),
        scratch_shapes=[
            VMEM((cells, channels), b2), VMEM((channels, channels), b2), VMEM((channels, channels), b2),
            VMEM((2, 3, 3, MAIN, channels), b2), VMEM((2, 3, 3, rest, channels), b2),
            VMEM((6, 3 * channels, 4 * rest), b2), VMEM((1, channels), f4),
            VMEM((cells, 128), b2), VMEM((channels, 512), b2),
            VMEM((1, channels), f4),
            VMEM(((height + 2) * width, 3 * channels), b2), VMEM((cells, channels), f4),
            VMEM((cells, half), b2), VMEM(piece, b2),
            VMEM((8, channels), f4), VMEM((2, 2, 128), f4), VMEM((2, n, 2, 128), f4),
            VMEM((2, height, 512), f4),
            VMEM((2, 2, width, 512), b2), VMEM((2, 2, height, 512), b2),
            VMEM((2, 2, width, 512), b2), VMEM((2, 2, height, 512), b2), VMEM((2, 4, 16, 512), b2),
            dma((chunks,)), dma((6,)), dma((2, jobs)), dma((2, jobs)), dma((chunks,)), dma((chunks,)), dma((chunks,)),
        ],
        compiler_params=pltpu.CompilerParams(
            collective_id=0, has_side_effects=True, vmem_limit_bytes=58 << 20
        ),
        name="block",
    )(timestep, mask, cloud_vec, norm_gain, x, time_weight[0], zero_weight, conv_weight[0])
    out = pl.pallas_call(
        merge_kernel,
        out_shape=bf16(cells, half),
        in_specs=[vmem] * 2,
        out_specs=hbm,
        scratch_shapes=[VMEM((cells, half), b2), dma((chunks,))],
        compiler_params=pltpu.CompilerParams(vmem_limit_bytes=8 << 20),
        name="merge",
    )(keep, got)
    return out.reshape(height, width, half)


def solution(mesh):
    return jax.shard_map(
        per_device,
        mesh=mesh,
        in_specs=(
            P("section", "gy", "gx", None),
            P("gy", "gx"),
            P(),
            P("section", None, None, None, None, None),
            P("section", None, None),
            P("section", None, None),
            P("section", None),
            P(),
        ),
        out_specs=P("gy", "gx", "section"),
        check_vma=False,
    )
```

```python
import functools
import math

import jax
import jax.numpy as jnp
from jax import lax
from jax.experimental import pallas as pl
from jax.experimental.pallas import tpu as pltpu
from jax.sharding import PartitionSpec as P

GROUPS = 32
EPS = 1e-05
ROWS = 8
MAIN = 256
SHARED = 2
MESH = pl.DeviceIdType.MESH
VMEM = pltpu.VMEM


def bf16(*shape):
    return jax.ShapeDtypeStruct(shape, jnp.bfloat16)


def add_cloud(x, m, cloud_ref):
    channels = x.shape[1]
    m = jnp.concatenate([m] * pl.cdiv(channels, 128), axis=1)[:, :channels]
    return x + m * cloud_ref[...]


def load_inputs(x_ref, mask_ref, cloud_ref, start, count):
    x = x_ref[pl.ds(start, count), :].astype(jnp.float32)
    return add_cloud(x, mask_ref[pl.ds(start, count), :].astype(jnp.float32), cloud_ref)


def merge_stats(stat_ref, t, index):
    cells = t.shape[0]
    mean = jnp.sum(t, axis=0, keepdims=True) / cells
    diff = t - mean
    square = jnp.sum(diff * diff, axis=0, keepdims=True)
    k = jnp.asarray(index, jnp.float32)
    delta = mean - stat_ref[0:1, :]
    stat_ref[0:1, :] = stat_ref[0:1, :] + delta / (k + 1.0)
    stat_ref[1:2, :] = stat_ref[1:2, :] + square + delta * delta * (cells * k / (k + 1.0))


def store_columns(t, width, stage_ref, lane, index):
    count = t.shape[1]
    t3 = t.reshape(ROWS, width, count)
    at = pl.ds(pl.multiple_of(index * ROWS, ROWS), ROWS)
    stage_ref[0, at, lane:lane + count] = t3[:, 0, :]
    stage_ref[1, at, lane:lane + count] = t3[:, width - 1, :]


def split_rows(v):
    high = v.astype(jnp.bfloat16)
    left = v - high.astype(jnp.float32)
    mid = left.astype(jnp.bfloat16)
    low = (left - mid.astype(jnp.float32)).astype(jnp.bfloat16)
    return high, mid, low


def exact_dot(rows, matrix):
    count = rows.shape[0]
    parts = jnp.concatenate([p.astype(jnp.float32) for p in split_rows(rows)], axis=0).astype(jnp.bfloat16)
    y = jnp.dot(parts, matrix, preferred_element_type=jnp.float32)
    return y[0:count] + (y[count:2 * count] + y[2 * count:3 * count])


def group_matrices(channels):
    per = channels // GROUPS

    def member(shape, axis):
        c = lax.broadcasted_iota(jnp.int32, shape, axis)
        g = lax.broadcasted_iota(jnp.int32, shape, 1 - axis)
        return jnp.where((c >= g * per) & (c < g * per + per), 1.0, 0.0).astype(jnp.bfloat16)

    return member((channels, 128), 0), member((128, channels), 1)


def pack_stats(stat_ref, send_ref, cells, matrices):
    to_group, to_channel = matrices
    channels = stat_ref.shape[1]
    per = channels // GROUPS
    mean, square = stat_ref[0:1, :], stat_ref[1:2, :]
    total = exact_dot(jnp.broadcast_to(mean, (8, channels)), to_group)
    off = mean - exact_dot(total / per, to_channel)[0:1, :]
    square = square + cells * off * off
    squares = exact_dot(jnp.broadcast_to(square, (8, channels)), to_group)
    row = lax.broadcasted_iota(jnp.int32, (8, 128), 0)
    send_ref[...] = jnp.where(row < 1, total / per, squares)[0:2, :]


def group_factors(g_ref, gain, cells, matrices):
    n = g_ref.shape[0]
    per = gain.shape[1] // GROUPS
    values = g_ref[...]
    sums = jnp.sum(values, axis=0)
    mean = jnp.broadcast_to(sums[0:1, :] / n, (8, 128))
    off = values - mean[None, 0:2]
    total = sums[1:2, :] + float(cells * per) * jnp.sum(off * off, axis=0)[0:1, :]
    inverse = jnp.broadcast_to(lax.rsqrt(total / (float(cells) * n * per) + EPS), (8, 128))
    return exact_dot(mean, matrices[1])[0:1, :], exact_dot(inverse, matrices[1])[0:1, :] * gain


def kernel(ny, nx, height, width, step_in, mask_in, cloud_in, gain_in, x_hbm, time_hbm, zero_hbm, w_hbm, keep_hbm, got_hbm,
           x_ref, time_ref, zero_ref, main_ref, rest_ref, side_ref, embed_ref,
           mask_ref, mix_ref, cloud_ref, q_ref, mid_ref, keep_ref, out_buf, stat_ref, stat_send, gathered,
           stage_ref, row_send, col_send, row_recv, col_recv, corner_recv, x_sem, w_sem, send, recv, keep_sem, swap_send, swap_recv,
           q2_ref, base_ref, mid_send, mid_recv, wx_send, wx_recv, wk_ref, wo_ref, line_send, line_recv, fac_send, fac_recv,
           cols_recv, top_recv, ends_recv, edge_ref, ex_send, ex_recv):
    me_s, me_y, me_x = lax.axis_index("section"), lax.axis_index("gy"), lax.axis_index("gx")
    n = ny * nx
    channels = x_ref.shape[1]
    half = keep_hbm.shape[1]
    cells = ROWS * width
    chunks = height // ROWS
    other = {"section": 1 - me_s}

    def near(dy, dx):
        return {"gy": lax.rem(me_y + dy + ny, ny), "gx": lax.rem(me_x + dx + nx, nx)}

    def load_x(i):
        at = pl.ds(pl.multiple_of(i * cells, cells), cells)
        return pltpu.make_async_copy(x_hbm.at[at], x_ref.at[at], x_sem.at[i])

    for i in range(chunks):
        load_x(i).start()
    rest = channels - MAIN
    loads = []
    for k in range(2):
        loads.append([
            pltpu.make_async_copy(w_hbm.at[k, :, :, pl.ds(0, MAIN)], main_ref.at[k], w_sem.at[2 * k]),
            pltpu.make_async_copy(w_hbm.at[k, :, :, pl.ds(MAIN, rest)], rest_ref.at[k], w_sem.at[2 * k + 1]),
        ])
    small = [
        pltpu.make_async_copy(time_hbm, time_ref, w_sem.at[4]),
        pltpu.make_async_copy(zero_hbm, zero_ref, w_sem.at[5]),
    ]
    for copy in small + loads[0] + loads[1]:
        copy.start()
    barrier = pltpu.get_barrier_semaphore()
    for d in range(1, n):
        pl.semaphore_signal(barrier, inc=1, device_id=near(d // nx, d % nx), device_id_type=MESH)
    pl.semaphore_signal(barrier, inc=1, device_id=other, device_id_type=MESH)
    cloud_ref[...] = cloud_in[...].astype(jnp.float32)
    gains = gain_in[0].astype(jnp.float32)
    matrices = group_matrices(channels)
    load = functools.partial(load_inputs, x_ref, mask_ref, cloud_ref)

    valid_up, valid_down = me_y > 0, me_y < ny - 1
    valid_left, valid_right = me_x > 0, me_x < nx - 1
    early = height - 16
    last_row = (height - 1) * width

    def remote(src, dst, sends, receives, target):
        return pltpu.make_async_remote_copy(
            src_ref=src, dst_ref=dst, send_sem=sends, recv_sem=receives,
            device_id=target, device_id_type=MESH,
        )

    def edge_jobs(phase):
        lanes = pl.ds(0, 512 if phase == 0 else 384)
        first, last = pl.ds(0, 16), pl.ds(width - 16, 16)
        up, down = valid_up, valid_down
        left, right = valid_left, valid_right
        rows, corner = row_send.at[phase], corner_recv.at[phase]
        cols = col_send.at[phase]
        jobs = []
        for side, dy, to, back in ((0, -1, up, down), (1, 1, down, up)):
            base = 0 if side else 1
            jobs.append((("row", side), rows.at[side, :, lanes], row_recv.at[phase, 1 - side, :, lanes], (dy, 0), to, back))
            jobs.append((("row", side), rows.at[side, last, lanes], corner.at[base, 0, :, lanes], (dy, 1), to & right, back & left))
            jobs.append((("row", side), rows.at[side, first, lanes], corner.at[base, 1, :, lanes], (dy, -1), to & left, back & right))
        for part, at in enumerate((pl.ds(0, early), pl.ds(early, 16))):
            jobs.append((("col", part), cols.at[1, at, lanes], col_recv.at[phase, 0, at, lanes], (0, 1), right, left))
            jobs.append((("col", part), cols.at[0, at, lanes], col_recv.at[phase, 1, at, lanes], (0, -1), left, right))
        return [
            (kind, functools.partial(remote, src, dst, send.at[phase, k], recv.at[phase, k], near(*step)), going, coming)
            for k, (kind, src, dst, step, going, coming) in enumerate(jobs)
        ]

    def start_edges(phase, *kinds):
        for kind, copy, going, _ in edge_jobs(phase):
            if kind in kinds:
                pl.when(going)(lambda: copy().start())

    def wait_edges(phase):
        for _, copy, going, coming in edge_jobs(phase):
            pl.when(going)(lambda: copy().wait_send())
            pl.when(coming)(lambda: copy().wait_recv())

    def pack_columns(phase, start, count):
        lanes = 512 if phase == 0 else 384
        for side in range(2):
            col_send[phase, side, start:start + count, 0:lanes] = stage_ref[side, start:start + count, 0:lanes].astype(jnp.bfloat16)

    def stat_copies(phase):
        order = sorted(range(1, n), key=lambda d: -min(d % nx, nx - d % nx))
        return [
            remote(stat_send.at[phase], gathered.at[phase, d], send.at[phase, 10 + d - 1], recv.at[phase, 10 + d - 1],
                   near(d // nx, d % nx))
            for d in order
        ]

    shared = SHARED * ROWS
    parity = lax.rem(me_y, 2)
    slots = 2 * nx
    share = wx_send.shape[0] // slots
    lanes = pl.ds(0, 384)

    def ship(k, src, dst, target=other):
        return remote(src, dst, ex_send.at[k], ex_recv.at[k], target)

    def slot(column, core):
        return pl.ds(pl.multiple_of((column * 2 + core) * share, 16), share)

    def weight_ship():
        at = slot(me_x, parity)
        return ship(0, wx_send.at[at], wx_recv.at[at])

    def column_ships():
        at = slot(me_x, parity)
        return [ship(d, wx_recv.at[at], wx_recv.at[at], near(0, d)) for d in range(1, nx)]

    def core_ships():
        sibling = {"gy": me_y + 1 - 2 * parity}
        return [ship(nx + d, wx_recv.at[slot(d, parity)], wx_recv.at[slot(d, parity)], sibling) for d in range(nx)]

    first_ship = 2 * nx

    def middle_ship(i):
        return ship(first_ship + i, mid_send.at[i], mid_recv.at[i])

    def line_ship():
        return ship(first_ship + SHARED, line_send, line_recv)

    def factor_ship():
        return ship(first_ship + SHARED + 1, fac_send, fac_recv)

    def border_ships():
        k = first_ship + SHARED + 2
        cols, ends = pl.ds(0, cols_recv.shape[1]), corner_recv
        return [
            (valid_left, lambda: ship(k, col_recv.at[1, 0, cols, lanes], cols_recv.at[0, :, :])),
            (valid_right, lambda: ship(k + 1, col_recv.at[1, 1, cols, lanes], cols_recv.at[1, :, :])),
            (valid_up, lambda: ship(k + 2, row_recv.at[1, 0, :, lanes], top_recv)),
            (valid_up & valid_left, lambda: ship(k + 3, ends.at[1, 0, 0, :, lanes], ends_recv.at[0])),
            (valid_up & valid_right, lambda: ship(k + 4, ends.at[1, 0, 1, :, lanes], ends_recv.at[1])),
        ]

    def pack_out(i, y):
        quarter = cells // 4
        out_buf[i, 0:cells, :] = y[:, 256:384].astype(jnp.bfloat16)
        out_buf[i, cells:cells + quarter, :] = fold(y[:, 384:512]).astype(jnp.bfloat16)

    def swap(i):
        return pltpu.make_async_remote_copy(
            src_ref=out_buf.at[i], dst_ref=got_hbm.at[i], send_sem=swap_send.at[i], recv_sem=swap_recv.at[i],
            device_id=other, device_id_type=MESH,
        )

    def share_weights():
        for copy in loads[1]:
            copy.wait()
        depth = 3 * channels
        for dy in range(3):
            w = jnp.concatenate(
                [main_ref[1, dy].reshape(3 * MAIN, channels), rest_ref[1, dy].reshape(3 * rest, channels)], axis=0
            )
            y = jnp.dot(w, mix_ref[...], preferred_element_type=jnp.float32)
            wk_ref[dy] = y[:, :half].astype(jnp.bfloat16)
            wx_send[dy * depth:(dy + 1) * depth, :] = y[:, 256:384].astype(jnp.bfloat16)
            at = 3 * depth + dy * depth // 4
            wx_send[at:at + depth // 4, :] = fold(y[:, 384:512]).astype(jnp.bfloat16)
        weight_ship().start()

    def share_inputs():
        for i in range(SHARED):
            t = load(i * cells, cells).astype(jnp.bfloat16)
            y = jnp.dot(t, mix_ref[...], preferred_element_type=jnp.float32)
            base_ref[i * cells:(i + 1) * cells, :] = y[:, :half]
            pack_out(i, y)
            swap(i).start()

    def share_middle(i):
        v = mid_ref[i * cells:(i + 1) * cells, :] - embed_ref[...]
        mid_send[i, 0:cells, :] = v[:, 0:128].astype(jnp.bfloat16)
        mid_send[i, cells:2 * cells, :] = v[:, 128:256].astype(jnp.bfloat16)
        tail = jnp.concatenate([v[:cells // 2, 256:], v[cells // 2:, 256:]], axis=1)
        mid_send[i, 2 * cells:, :] = tail.astype(jnp.bfloat16)
        middle_ship(i).start()

    def share_line():
        v = mid_ref[shared * width:(shared + 1) * width, :] - embed_ref[...]
        line_send[:, 0:channels] = v.astype(jnp.bfloat16)
        line_ship().start()

    def share_factors(mean, scale):
        fac_send[0:1, 0:channels] = mean - embed_ref[...]
        fac_send[1:2, 0:channels] = scale
        factor_ship().start()
        for valid, copy in border_ships():
            pl.when(valid)(lambda: copy().start())

    def gather_shared():
        for copy in core_ships() + [middle_ship(i) for i in range(SHARED)] + [line_ship(), factor_ship()]:
            copy.wait()
        for valid, copy in border_ships():
            pl.when(valid)(lambda: copy().wait())
        depth = 3 * channels
        for dy in range(3):
            wo_ref[dy, :, 0:128] = wx_recv[dy * depth:(dy + 1) * depth, :]
            at = 3 * depth + dy * depth // 4
            tail = wx_recv[at:at + depth // 4, :]
            for k in range(4):
                wo_ref[dy, k * depth // 4:(k + 1) * depth // 4, 128:half] = tail[:, 32 * k:32 * k + 32]

    def exchange(phase, send_edges, meanwhile):
        pack_stats(stat_ref, stat_send.at[phase], height * width, matrices)
        if phase == 0:
            pl.semaphore_wait(barrier, n)
        for copy in stat_copies(phase):
            copy.start()
        send_edges()
        gathered[phase, 0] = stat_send[phase]
        if phase == 0:
            for copy in loads[0]:
                copy.wait()
        fill_sides(main_ref.at[phase], rest_ref.at[phase], side_ref)
        meanwhile()
        for copy in stat_copies(phase):
            copy.wait()
        factors = group_factors(gathered.at[phase], gains[phase:phase + 1], height * width, matrices)
        wait_edges(phase)
        return factors

    def activate(mean, scale):
        half_scale = scale * 0.5

        def act(t, valid=None):
            z = (t - mean) * half_scale
            z = z + z * jnp.tanh(z)
            return z if valid is None else jnp.where(valid, z, 0.0)

        return act

    def filler(phase, source, mean, scale):
        act = activate(mean, scale)

        def border_act(v, valid):
            v = v.astype(jnp.float32)
            if phase == 0:
                t = add_cloud(v[:, :channels], v[:, 384:512], cloud_ref)
            else:
                t = v[:, :channels] + embed_ref[...]
            return act(t, valid)

        stage_ref[0, :, 0:channels] = border_act(col_recv[phase, 0], valid_left)
        stage_ref[1, :, 0:channels] = border_act(col_recv[phase, 1], valid_right)

        def chunk(i, count=ROWS):
            at = pl.ds(pl.multiple_of(i * ROWS, ROWS), count)
            fill_columns(
                q_ref, pl.multiple_of(i * cells + width, width),
                act(source(pl.multiple_of(i * cells, cells), count * width)),
                stage_ref[0, at, 0:channels], stage_ref[1, at, 0:channels], count, width,
            )

        def line(r):
            fill_columns(
                q_ref, (r + 1) * width, act(source(r * width, width)),
                stage_ref[0, r:r + 1, 0:channels], stage_ref[1, r:r + 1, 0:channels], 1, width,
            )

        def border(k):
            lcol = border_act(corner_recv[phase, k, 0], valid_left & (valid_down if k else valid_up))[15:16, :]
            rcol = border_act(corner_recv[phase, k, 1], valid_right & (valid_down if k else valid_up))[0:1, :]
            fill_columns(
                q_ref, (height + 1) * width if k else 0, border_act(row_recv[phase, k], valid_down if k else valid_up),
                lcol, rcol, 1, width,
            )

        return chunk, line, border

    def run(chunk, step, begin, after=None):
        def body(i, carry):
            chunk(i + 1)
            step(i)
            if after is not None:
                after(i)
            return carry

        lax.fori_loop(begin, chunks - 1, body, 0)

    stat_ref[...] = jnp.zeros_like(stat_ref)
    ones = lax.broadcasted_iota(jnp.int32, (ROWS, ROWS * 128), 1) // 128
    ones = (ones == lax.broadcasted_iota(jnp.int32, (ROWS, ROWS * 128), 0)).astype(jnp.float32).astype(jnp.bfloat16)

    def spread_mask(i, carry):
        m = mask_in[pl.ds(pl.multiple_of(i * ROWS, ROWS), ROWS), :].astype(jnp.float32).astype(jnp.bfloat16)
        wide = lax.dot_general(m, ones, (((0,), (0,)), ((), ())), preferred_element_type=jnp.float32)
        for r in range(ROWS):
            at = pl.ds(pl.multiple_of(i * cells + r * width, width), width)
            mask_ref[at, :] = wide[:, r * 128:(r + 1) * 128].astype(jnp.bfloat16)
        return carry

    lax.fori_loop(0, chunks, spread_mask, 0)
    for copy in small:
        copy.wait()
    angles = lax.broadcasted_iota(jnp.int32, (16, half), 1).astype(jnp.float32)
    angles = step_in[0].astype(jnp.float32) * jnp.exp(-math.log(10000.0) * angles / half)
    embed = sum(
        jnp.dot(wave(angles).astype(jnp.bfloat16), time_ref[k * half:(k + 1) * half, :], preferred_element_type=jnp.float32)
        for k, wave in enumerate((jnp.cos, jnp.sin))
    )[0:1, :]
    embed_ref[...] = embed / (1.0 + jnp.exp(-embed))
    zero = zero_ref[...].astype(jnp.float32)
    line = lax.broadcasted_iota(jnp.int32, (channels, 1), 0)

    def place(start, stop, count, repeat):
        lane = lax.broadcasted_iota(jnp.int32, (channels, count), 1)
        shift = (stop + half) % channels
        unit = jnp.where(line == lane + shift, 1.0, 0.0)
        part = jnp.where(me_s == 0, zero[:, stop:stop + count], unit).astype(jnp.float32)
        part = jnp.concatenate([part] * repeat, axis=1) if repeat > 1 else part
        mix_ref[:, start:start + count * repeat] = part.astype(jnp.bfloat16)

    mix_ref[:, 128:256] = jnp.zeros((channels, 128), jnp.bfloat16)
    place(0, 0, half, 1)
    place(256, half, 128, 1)
    place(384, half + 128, 32, 4)

    def first_stats(i, carry):
        load_x(i).wait()
        at = pl.ds(pl.multiple_of(i * cells, cells), cells)
        x, m = x_ref[at, :].astype(jnp.float32), mask_ref[at, :].astype(jnp.float32)
        store_columns(x, width, stage_ref, 0, i)
        store_columns(m, width, stage_ref, 384, i)
        merge_stats(stat_ref, add_cloud(x, m, cloud_ref), i)
        return carry

    lax.fori_loop(0, chunks, first_stats, 0)
    pack_columns(0, 0, height)
    for side, start in ((0, 0), (1, last_row)):
        row_send[0, side, :, 0:channels] = x_ref[start:start + width, :]
        row_send[0, side, :, 384:512] = mask_ref[start:start + width, :]

    def prepare():
        share_weights()
        share_inputs()

    factors = exchange(0, lambda: start_edges(0, ("row", 0), ("row", 1), ("col", 0), ("col", 1)), prepare)
    stat_ref[...] = jnp.zeros_like(stat_ref)

    def first_step(i):
        t = conv_chunk(q_ref, main_ref.at[0], rest_ref.at[0], side_ref, i, width)
        store_columns(t, width, stage_ref, 0, i)
        t = t + embed_ref[...]
        mid_ref[pl.ds(pl.multiple_of(i * cells, cells), cells), :] = t
        merge_stats(stat_ref, t, i)

    def send_row(side, start):
        row_send[1, side, :, 0:channels] = (mid_ref[start:start + width, :] - embed_ref[...]).astype(jnp.bfloat16)
        start_edges(1, ("row", side))

    def send_early():
        pack_columns(1, 0, early)
        start_edges(1, ("col", 0))

    def after_step(i):
        @pl.when(i == SHARED)
        def _():
            for k in range(1, SHARED):
                share_middle(k)
            share_line()

    chunk, _, border = filler(0, load, *factors)
    border(0)
    border(1)
    chunk(0)
    chunk(1)
    first_step(0)
    send_row(0, 0)
    share_middle(0)
    weight_ship().wait()
    for copy in column_ships():
        copy.start()
    run(chunk, first_step, 1, after_step)
    send_early()
    first_step(chunks - 1)

    def send_late():
        pack_columns(1, early, 16)
        start_edges(1, ("col", 1))
        send_row(1, last_row)

    def pass_weights():
        for copy in column_ships():
            copy.wait()
        for copy in core_ships():
            copy.start()

    factors = exchange(1, send_late, pass_weights)
    share_factors(*factors)
    def store_keep(i):
        at = pl.ds(pl.multiple_of(i * cells, cells), cells)
        return pltpu.make_async_copy(keep_ref.at[at], keep_hbm.at[at], keep_sem.at[i])

    def second_step(i):
        at = pl.ds(pl.multiple_of(i * cells, cells), cells)
        t = load(pl.multiple_of(i * cells, cells), cells)
        skip = (t + conv_chunk(q_ref, main_ref.at[1], rest_ref.at[1], side_ref, i, width)).astype(jnp.bfloat16)
        y = jnp.dot(skip, mix_ref[...], preferred_element_type=jnp.float32)
        pack_out(i, y)
        swap(i).start()
        keep_ref[at, :] = y[:, :half].astype(jnp.bfloat16)
        store_keep(i).start()

    chunk, line, border = filler(1, lambda s, c: mid_ref[pl.ds(s, c), :], *factors)
    line(shared - 1)
    chunk(SHARED)
    run(chunk, second_step, SHARED)
    border(1)
    second_step(chunks - 1)

    border(0)
    gather_shared()
    act = activate(fac_recv[0:1, 0:channels], fac_recv[1:2, 0:channels])

    def unpack(v):
        return v.astype(jnp.float32)[:, :channels]

    edge_ref[0] = act(unpack(cols_recv[0]), valid_left)
    edge_ref[1] = act(unpack(cols_recv[1]), valid_right)
    lcol = act(unpack(ends_recv[0]), valid_up & valid_left)[15:16, :]
    rcol = act(unpack(ends_recv[1]), valid_up & valid_right)[0:1, :]
    fill_columns(q2_ref, 0, act(unpack(top_recv[...]), valid_up), lcol, rcol, 1, width)
    fill_columns(
        q2_ref, (shared + 1) * width, act(unpack(line_recv[...])),
        edge_ref[0, shared:shared + 1, :], edge_ref[1, shared:shared + 1, :], 1, width,
    )

    def shared_fill(i, carry):
        chunk(i)
        tail = mid_recv[i, 2 * cells:, :].astype(jnp.float32)
        tail = jnp.concatenate([tail[:, 0:64], tail[:, 64:128]], axis=0)
        v = [mid_recv[i, k * cells:(k + 1) * cells, :].astype(jnp.float32) for k in range(2)]
        at = pl.ds(pl.multiple_of(i * ROWS, ROWS), ROWS)
        fill_columns(
            q2_ref, pl.multiple_of(i * cells + width, width), act(jnp.concatenate(v + [tail], axis=1)),
            edge_ref[0, at, :], edge_ref[1, at, :], ROWS, width,
        )
        return carry

    lax.fori_loop(0, SHARED, shared_fill, 0)

    def shared_step(i, carry):
        at = pl.ds(pl.multiple_of(i * cells, cells), cells)
        t = base_ref[at, :]
        for source, w_ref in ((q_ref, wk_ref), (q2_ref, wo_ref)):
            for dy in range(3):
                a = source[pl.ds(pl.multiple_of((i * ROWS + dy) * width, width), cells), :]
                t = t + jnp.dot(a, w_ref[dy], preferred_element_type=jnp.float32)
        keep_ref[at, :] = t.astype(jnp.bfloat16)
        store_keep(i).start()
        return carry

    lax.fori_loop(0, SHARED, shared_step, 0)

    def finish(i, carry):
        store_keep(i).wait()
        swap(i).wait()
        return carry

    lax.fori_loop(0, chunks, finish, 0)


def fold(y):
    quarter = y.shape[0] // 4
    lane = lax.broadcasted_iota(jnp.int32, (quarter, 128), 1)
    rest = y[0:quarter]
    for k in range(1, 4):
        rest = jnp.where(lane >= 32 * k, y[k * quarter:(k + 1) * quarter], rest)
    return rest


def merge_kernel(keep_ref, got_ref, out_hbm, out_ref, sem):
    chunks, cells = got_ref.shape[0], keep_ref.shape[0] // got_ref.shape[0]
    quarter = cells // 4

    def store(i):
        at = pl.ds(pl.multiple_of(i * cells, cells), cells)
        return pltpu.make_async_copy(out_ref.at[at], out_hbm.at[at], sem.at[i])

    def merge(i, carry):
        rest = got_ref[i, cells:, :].astype(jnp.float32)
        for k in range(4):
            got = got_ref[i, k * quarter:(k + 1) * quarter, :].astype(jnp.float32)
            got = jnp.concatenate([got, rest[:, 32 * k:32 * k + 32]], axis=1)
            at = pl.ds(pl.multiple_of(i * cells + k * quarter, quarter), quarter)
            out_ref[at, :] = (keep_ref[at, :].astype(jnp.float32) + got).astype(jnp.bfloat16)
        store(i).start()
        return carry

    lax.fori_loop(0, chunks, merge, 0)

    def finish(i, carry):
        store(i).wait()
        return carry

    lax.fori_loop(0, chunks, finish, 0)


def fill_columns(q_ref, start, act, lcol, rcol, rows, width):
    channels = act.shape[1]
    v = act.reshape(rows, width, channels)
    col = lax.broadcasted_iota(jnp.int32, v.shape, 1)
    vl = jnp.where(col == 0, lcol.reshape(rows, 1, channels), pltpu.roll(v, 1, 1))
    vr = jnp.where(col == width - 1, rcol.reshape(rows, 1, channels), pltpu.roll(v, width - 1, 1))
    at = pl.ds(start, rows * width)
    parts = [p.reshape(rows * width, channels) for p in (vl, v, vr)]
    for k, part in enumerate(parts):
        q_ref[at, k * MAIN:(k + 1) * MAIN] = part[:, :MAIN].astype(jnp.bfloat16)
    tails = [p[:, MAIN:] for p in parts]
    q_ref[at, 3 * MAIN:] = jnp.concatenate(tails, axis=1).astype(jnp.bfloat16)


def fill_sides(main_ref, rest_ref, side_ref):
    rest = side_ref.shape[2] // 4
    blank = jnp.zeros((3 * MAIN, rest), jnp.bfloat16)
    for r in range(6):
        top, low = [], []
        for k in range(4):
            dy = r - k
            inside = 0 <= dy <= 2
            top.append(main_ref[dy, :, :, MAIN:].reshape(3 * MAIN, rest) if inside else blank)
            low.append(rest_ref[dy, :, :, MAIN:].reshape(3 * rest, rest) if inside else blank[:3 * rest])
        side_ref[r, 0:3 * MAIN, :] = jnp.concatenate(top, axis=1)
        side_ref[r, 3 * MAIN:, :] = jnp.concatenate(low, axis=1)


def conv_chunk(q_ref, main_ref, rest_ref, side_ref, i, width):
    cells = ROWS * width
    rest = rest_ref.shape[2]

    def rows(start, count):
        return q_ref[pl.ds(pl.multiple_of((i * ROWS + start) * width, width), count * width), :]

    total = None
    for dy in range(3):
        w = jnp.concatenate(
            [main_ref[dy, :, :, 0:MAIN].reshape(3 * MAIN, MAIN), rest_ref[dy, :, :, 0:MAIN].reshape(3 * rest, MAIN)], axis=0
        )
        part = jnp.dot(rows(dy, ROWS), w, preferred_element_type=jnp.float32)
        total = part if total is None else total + part
    side = None
    for r in range(6):
        a = jnp.concatenate([rows(4 * k + r, 1) for k in range(ROWS // 4)], axis=0)
        part = jnp.dot(a, side_ref[r], preferred_element_type=jnp.float32)
        side = part if side is None else side + part
    side = jnp.concatenate(
        [side[k * width:(k + 1) * width, j * rest:(j + 1) * rest] for k in range(ROWS // 4) for j in range(4)], axis=0
    )
    return jnp.concatenate([total, side], axis=1)


def per_device(streams, mask, timestep, conv_weight, norm_gain, time_weight, cloud_vec, zero_weight):
    ny, nx = lax.axis_size("gy"), lax.axis_size("gx")
    height, width, channels = streams.shape[1:]
    cells = height * width
    half = channels // 2
    x = streams.reshape(cells, channels)
    n = ny * nx
    rest = channels - MAIN
    chunks = height // ROWS
    piece = (chunks, ROWS * width * 5 // 4, 128)
    jobs = n - 1 + 10
    shared = SHARED * ROWS
    share = pl.cdiv(9 * channels * 5 // 4, 32 * nx) * 16
    dma = pltpu.SemaphoreType.DMA
    vmem = pl.BlockSpec(memory_space=VMEM)
    hbm = pl.BlockSpec(memory_space=pltpu.HBM)
    either = pl.BlockSpec(memory_space=pl.ANY)
    f4, b2 = jnp.float32, jnp.bfloat16
    keep, got = pl.pallas_call(
        functools.partial(kernel, ny, nx, height, width),
        out_shape=(VMEM((cells, half), b2), VMEM(piece, b2)),
        in_specs=[pl.BlockSpec(memory_space=pltpu.SMEM)] + [vmem] * 3 + [hbm] * 4,
        out_specs=(either, either),
        scratch_shapes=[
            VMEM((cells, channels), b2), VMEM((channels, channels), b2), VMEM((channels, channels), b2),
            VMEM((2, 3, 3, MAIN, channels), b2), VMEM((2, 3, 3, rest, channels), b2),
            VMEM((6, 3 * channels, 4 * rest), b2), VMEM((1, channels), f4),
            VMEM((cells, 128), b2), VMEM((channels, 512), b2),
            VMEM((1, channels), f4),
            VMEM(((height + 2) * width, 3 * channels), b2), VMEM((cells, channels), f4),
            VMEM((cells, half), b2), VMEM(piece, b2),
            VMEM((8, channels), f4), VMEM((2, 2, 128), f4), VMEM((2, n, 2, 128), f4),
            VMEM((2, height, 512), f4),
            VMEM((2, 2, width, 512), b2), VMEM((2, 2, height, 512), b2),
            VMEM((2, 2, width, 512), b2), VMEM((2, 2, height, 512), b2), VMEM((2, 2, 2, 16, 512), b2),
            dma((chunks,)), dma((6,)), dma((2, jobs)), dma((2, jobs)), dma((chunks,)), dma((chunks,)), dma((chunks,)),
            VMEM(((shared + 2) * width, 3 * channels), b2), VMEM((shared * width, half), f4),
            VMEM((SHARED, ROWS * width * 5 // 2, 128), b2), VMEM((SHARED, ROWS * width * 5 // 2, 128), b2),
            VMEM((2 * nx * share, 128), b2), VMEM((2 * nx * share, 128), b2),
            VMEM((3, 3 * channels, half), b2), VMEM((3, 3 * channels, half), b2),
            VMEM((width, 384), b2), VMEM((width, 384), b2), VMEM((2, 384), f4), VMEM((2, 384), f4),
            VMEM((2, shared + 16, 384), b2), VMEM((width, 384), b2), VMEM((2, 16, 384), b2),
            VMEM((2, shared + 16, channels), f4), dma((2 * nx + SHARED + 7,)), dma((2 * nx + SHARED + 7,)),
        ],
        compiler_params=pltpu.CompilerParams(
            collective_id=0, has_side_effects=True, vmem_limit_bytes=58 << 20
        ),
        name="block",
    )(timestep, mask, cloud_vec, norm_gain, x, time_weight[0], zero_weight, conv_weight[0])
    out = pl.pallas_call(
        merge_kernel,
        out_shape=bf16(cells, half),
        in_specs=[vmem] * 2,
        out_specs=hbm,
        scratch_shapes=[VMEM((cells, half), b2), dma((chunks,))],
        compiler_params=pltpu.CompilerParams(vmem_limit_bytes=8 << 20),
        name="merge",
    )(keep, got)
    return out.reshape(height, width, half)


def solution(mesh):
    return jax.shard_map(
        per_device,
        mesh=mesh,
        in_specs=(
            P("section", "gy", "gx", None),
            P("gy", "gx"),
            P(),
            P("section", None, None, None, None, None),
            P("section", None, None),
            P("section", None, None),
            P("section", None),
            P(),
        ),
        out_specs=P("gy", "gx", "section"),
        check_vma=False,
    )
```

```python
import functools
import math

import jax
import jax.numpy as jnp
from jax import lax
from jax.experimental import pallas as pl
from jax.experimental.pallas import tpu as pltpu
from jax.sharding import PartitionSpec as P

GROUPS = 32
EPS = 1e-05
ROWS = 8
MAIN = 256
SHARED = 2
MESH = pl.DeviceIdType.MESH
VMEM = pltpu.VMEM


def bf16(*shape):
    return jax.ShapeDtypeStruct(shape, jnp.bfloat16)


def add_cloud(x, m, cloud_ref):
    channels = x.shape[1]
    m = jnp.concatenate([m] * pl.cdiv(channels, 128), axis=1)[:, :channels]
    return x + m * cloud_ref[...]


def load_inputs(x_ref, mask_ref, cloud_ref, start, count):
    x = x_ref[pl.ds(start, count), :].astype(jnp.float32)
    return add_cloud(x, mask_ref[pl.ds(start, count), :].astype(jnp.float32), cloud_ref)


def merge_stats(stat_ref, t, index):
    cells = t.shape[0]
    mean = jnp.sum(t, axis=0, keepdims=True) / cells
    diff = t - mean
    square = jnp.sum(diff * diff, axis=0, keepdims=True)
    k = jnp.asarray(index, jnp.float32)
    delta = mean - stat_ref[0:1, :]
    stat_ref[0:1, :] = stat_ref[0:1, :] + delta / (k + 1.0)
    stat_ref[1:2, :] = stat_ref[1:2, :] + square + delta * delta * (cells * k / (k + 1.0))


def store_columns(t, width, stage_ref, lane, index):
    count = t.shape[1]
    t3 = t.reshape(ROWS, width, count)
    at = pl.ds(pl.multiple_of(index * ROWS, ROWS), ROWS)
    stage_ref[0, at, lane:lane + count] = t3[:, 0, :]
    stage_ref[1, at, lane:lane + count] = t3[:, width - 1, :]


def split_rows(v):
    high = v.astype(jnp.bfloat16)
    left = v - high.astype(jnp.float32)
    mid = left.astype(jnp.bfloat16)
    low = (left - mid.astype(jnp.float32)).astype(jnp.bfloat16)
    return high, mid, low


def exact_dot(rows, matrix):
    count = rows.shape[0]
    parts = jnp.concatenate([p.astype(jnp.float32) for p in split_rows(rows)], axis=0).astype(jnp.bfloat16)
    y = jnp.dot(parts, matrix, preferred_element_type=jnp.float32)
    return y[0:count] + (y[count:2 * count] + y[2 * count:3 * count])


def group_matrices(channels):
    per = channels // GROUPS

    def member(shape, axis):
        c = lax.broadcasted_iota(jnp.int32, shape, axis)
        g = lax.broadcasted_iota(jnp.int32, shape, 1 - axis)
        return jnp.where((c >= g * per) & (c < g * per + per), 1.0, 0.0).astype(jnp.bfloat16)

    return member((channels, 128), 0), member((128, channels), 1)


def pack_stats(stat_ref, send_ref, cells, matrices):
    to_group, to_channel = matrices
    channels = stat_ref.shape[1]
    per = channels // GROUPS
    mean, square = stat_ref[0:1, :], stat_ref[1:2, :]
    total = exact_dot(jnp.broadcast_to(mean, (8, channels)), to_group)
    off = mean - exact_dot(total / per, to_channel)[0:1, :]
    square = square + cells * off * off
    squares = exact_dot(jnp.broadcast_to(square, (8, channels)), to_group)
    row = lax.broadcasted_iota(jnp.int32, (8, 128), 0)
    send_ref[...] = jnp.where(row < 1, total / per, squares)[0:2, :]


def group_factors(g_ref, gain, cells, matrices):
    n = g_ref.shape[0]
    per = gain.shape[1] // GROUPS
    values = g_ref[...]
    sums = jnp.sum(values, axis=0)
    mean = jnp.broadcast_to(sums[0:1, :] / n, (8, 128))
    off = values - mean[None, 0:2]
    total = sums[1:2, :] + float(cells * per) * jnp.sum(off * off, axis=0)[0:1, :]
    inverse = jnp.broadcast_to(lax.rsqrt(total / (float(cells) * n * per) + EPS), (8, 128))
    return exact_dot(mean, matrices[1])[0:1, :], exact_dot(inverse, matrices[1])[0:1, :] * gain


def kernel(ny, nx, height, width, step_in, mask_in, cloud_in, gain_in, x_hbm, time_hbm, zero_hbm, w_hbm, keep_hbm, got_hbm,
           x_ref, time_ref, zero_ref, main_ref, rest_ref, side_ref, embed_ref,
           mask_ref, mix_ref, cloud_ref, qa_ref, qb_ref, halo_ref, mid_ref, keep_ref, out_buf, stat_ref, stat_send, gathered,
           stage_ref, row_send, col_send, row_recv, col_recv, corner_recv, x_sem, w_sem, send, recv, keep_sem, swap_send, swap_recv,
           q2_ref, base_ref, mid_send, mid_recv, wx_send, wx_recv, wk_ref, wo_ref, line_send, line_recv, fac_send, fac_recv,
           cols_recv, top_recv, ends_recv, edge_ref, ex_send, ex_recv):
    me_s, me_y, me_x = lax.axis_index("section"), lax.axis_index("gy"), lax.axis_index("gx")
    n = ny * nx
    channels = x_ref.shape[1]
    half = keep_hbm.shape[1]
    cells = ROWS * width
    chunks = height // ROWS
    other = {"section": 1 - me_s}

    def near(dy, dx):
        return {"gy": lax.rem(me_y + dy + ny, ny), "gx": lax.rem(me_x + dx + nx, nx)}

    def load_x(i):
        at = pl.ds(i * cells if isinstance(i, int) else pl.multiple_of(i * cells, cells), cells)
        return pltpu.make_async_copy(x_hbm.at[at], x_ref.at[at], x_sem.at[i])

    for i in range(chunks):
        load_x(i).start()
    rest = channels - MAIN
    loads = []
    for k in range(2):
        loads.append([
            pltpu.make_async_copy(w_hbm.at[k, :, :, pl.ds(0, MAIN)], main_ref.at[k], w_sem.at[2 * k]),
            pltpu.make_async_copy(w_hbm.at[k, :, :, pl.ds(MAIN, rest)], rest_ref.at[k], w_sem.at[2 * k + 1]),
        ])
    small = [
        pltpu.make_async_copy(time_hbm, time_ref, w_sem.at[4]),
        pltpu.make_async_copy(zero_hbm, zero_ref, w_sem.at[5]),
    ]
    for copy in small + loads[0] + loads[1]:
        copy.start()
    barrier = pltpu.get_barrier_semaphore()
    for d in range(1, n):
        pl.semaphore_signal(barrier, inc=1, device_id=near(d // nx, d % nx), device_id_type=MESH)
    pl.semaphore_signal(barrier, inc=1, device_id=other, device_id_type=MESH)
    cloud_ref[...] = cloud_in[...].astype(jnp.float32)
    gains = gain_in[0].astype(jnp.float32)
    matrices = group_matrices(channels)
    load = functools.partial(load_inputs, x_ref, mask_ref, cloud_ref)

    valid_up, valid_down = me_y > 0, me_y < ny - 1
    valid_left, valid_right = me_x > 0, me_x < nx - 1
    early = height - 16
    last_row = (height - 1) * width

    def remote(src, dst, sends, receives, target):
        return pltpu.make_async_remote_copy(
            src_ref=src, dst_ref=dst, send_sem=sends, recv_sem=receives,
            device_id=target, device_id_type=MESH,
        )

    def edge_jobs(phase):
        lanes = pl.ds(0, 512 if phase == 0 else 384)
        first, last = pl.ds(0, 16), pl.ds(width - 16, 16)
        up, down = valid_up, valid_down
        left, right = valid_left, valid_right
        rows, corner = row_send.at[phase], corner_recv.at[phase]
        cols = col_send.at[phase]
        jobs = []
        for side, dy, to, back in ((0, -1, up, down), (1, 1, down, up)):
            base = 0 if side else 1
            jobs.append((("row", side), rows.at[side, :, lanes], row_recv.at[phase, 1 - side, :, lanes], (dy, 0), to, back))
            jobs.append((("row", side), rows.at[side, last, lanes], corner.at[base, 0, :, lanes], (dy, 1), to & right, back & left))
            jobs.append((("row", side), rows.at[side, first, lanes], corner.at[base, 1, :, lanes], (dy, -1), to & left, back & right))
        for part, at in enumerate((pl.ds(0, early), pl.ds(early, 16))):
            jobs.append((("col", part), cols.at[1, at, lanes], col_recv.at[phase, 0, at, lanes], (0, 1), right, left))
            jobs.append((("col", part), cols.at[0, at, lanes], col_recv.at[phase, 1, at, lanes], (0, -1), left, right))
        return [
            (kind, functools.partial(remote, src, dst, send.at[phase, k], recv.at[phase, k], near(*step)), going, coming)
            for k, (kind, src, dst, step, going, coming) in enumerate(jobs)
        ]

    def start_edges(phase, *kinds):
        for kind, copy, going, _ in edge_jobs(phase):
            if kind in kinds:
                pl.when(going)(lambda: copy().start())

    def wait_edges(phase):
        for _, copy, going, coming in edge_jobs(phase):
            pl.when(going)(lambda: copy().wait_send())
            pl.when(coming)(lambda: copy().wait_recv())

    def pack_columns(phase, start, count):
        at = slice(start, start + count)
        for side in range(2):
            if phase == 0:
                col_send[0, side, at, :] = stage_ref[side, at, :].astype(jnp.bfloat16)
            else:
                t = stage_ref[side, at, 0:channels] - embed_ref[...]
                col_send[1, side, at, 0:channels] = t.astype(jnp.bfloat16)

    def stat_copies(phase):
        order = sorted(range(1, n), key=lambda d: -min(d % nx, nx - d % nx))
        return [
            remote(stat_send.at[phase], gathered.at[phase, d], send.at[phase, 10 + d - 1], recv.at[phase, 10 + d - 1],
                   near(d // nx, d % nx))
            for d in order
        ]

    shared = SHARED * ROWS
    parity = lax.rem(me_y, 2)
    slots = 2 * nx
    share = wx_send.shape[0] // slots
    lanes = pl.ds(0, 384)

    def ship(k, src, dst, target=other):
        return remote(src, dst, ex_send.at[k], ex_recv.at[k], target)

    def slot(column, core):
        return pl.ds(pl.multiple_of((column * 2 + core) * share, 16), share)

    def weight_ship():
        at = slot(me_x, parity)
        return ship(0, wx_send.at[at], wx_recv.at[at])

    def column_ships():
        at = slot(me_x, parity)
        return [ship(d, wx_recv.at[at], wx_recv.at[at], near(0, d)) for d in range(1, nx)]

    def core_ships():
        sibling = {"gy": me_y + 1 - 2 * parity}
        return [ship(nx + d, wx_recv.at[slot(d, parity)], wx_recv.at[slot(d, parity)], sibling) for d in range(nx)]

    first_ship = 2 * nx

    def middle_ship(i):
        return ship(first_ship + i, mid_send.at[i], mid_recv.at[i])

    def line_ship():
        return ship(first_ship + SHARED, line_send, line_recv)

    def factor_ship():
        return ship(first_ship + SHARED + 1, fac_send, fac_recv)

    def border_ships():
        k = first_ship + SHARED + 2
        cols, ends = pl.ds(0, cols_recv.shape[1]), corner_recv
        return [
            (valid_left, lambda: ship(k, col_recv.at[1, 0, cols, lanes], cols_recv.at[0, :, :])),
            (valid_right, lambda: ship(k + 1, col_recv.at[1, 1, cols, lanes], cols_recv.at[1, :, :])),
            (valid_up, lambda: ship(k + 2, row_recv.at[1, 0, :, lanes], top_recv)),
            (valid_up & valid_left, lambda: ship(k + 3, ends.at[1, 0, 0, :, lanes], ends_recv.at[0])),
            (valid_up & valid_right, lambda: ship(k + 4, ends.at[1, 0, 1, :, lanes], ends_recv.at[1])),
        ]

    def pack_out(i, y):
        quarter = cells // 4
        out_buf[i, 0:cells, :] = y[:, 256:384].astype(jnp.bfloat16)
        out_buf[i, cells:cells + quarter, :] = fold(y[:, 384:512]).astype(jnp.bfloat16)

    def swap(i):
        return pltpu.make_async_remote_copy(
            src_ref=out_buf.at[i], dst_ref=got_hbm.at[i], send_sem=swap_send.at[i], recv_sem=swap_recv.at[i],
            device_id=other, device_id_type=MESH,
        )

    def share_weights():
        for copy in loads[1]:
            copy.wait()
        depth = 3 * channels
        for dy in range(3):
            w = jnp.concatenate(
                [main_ref[1, dy].reshape(3 * MAIN, channels), rest_ref[1, dy].reshape(3 * rest, channels)], axis=0
            )
            y = jnp.dot(w, mix_ref[...], preferred_element_type=jnp.float32)
            wk_ref[dy] = y[:, :half].astype(jnp.bfloat16)
            wx_send[dy * depth:(dy + 1) * depth, :] = y[:, 256:384].astype(jnp.bfloat16)
            at = 3 * depth + dy * depth // 4
            wx_send[at:at + depth // 4, :] = fold(y[:, 384:512]).astype(jnp.bfloat16)
        weight_ship().start()

    def share_inputs():
        for i in range(SHARED):
            t = load(i * cells, cells).astype(jnp.bfloat16)
            y = jnp.dot(t, mix_ref[...], preferred_element_type=jnp.float32)
            base_ref[i * cells:(i + 1) * cells, :] = y[:, :half]
            pack_out(i, y)
            swap(i).start()

    def share_middle(i):
        v = mid_ref[i * cells:(i + 1) * cells, :] - embed_ref[...]
        mid_send[i, 0:cells, :] = v[:, 0:128].astype(jnp.bfloat16)
        mid_send[i, cells:2 * cells, :] = v[:, 128:256].astype(jnp.bfloat16)
        tail = jnp.concatenate([v[:cells // 2, 256:], v[cells // 2:, 256:]], axis=1)
        mid_send[i, 2 * cells:, :] = tail.astype(jnp.bfloat16)
        middle_ship(i).start()

    def share_line():
        v = mid_ref[shared * width:(shared + 1) * width, :] - embed_ref[...]
        line_send[:, 0:channels] = v.astype(jnp.bfloat16)
        line_ship().start()

    def share_factors(mean, scale):
        fac_send[0:1, 0:channels] = mean - embed_ref[...]
        fac_send[1:2, 0:channels] = scale
        factor_ship().start()
        for valid, copy in border_ships():
            pl.when(valid)(lambda: copy().start())

    def gather_shared():
        for copy in core_ships() + [middle_ship(i) for i in range(SHARED)] + [line_ship(), factor_ship()]:
            copy.wait()
        for valid, copy in border_ships():
            pl.when(valid)(lambda: copy().wait())
        depth = 3 * channels
        for dy in range(3):
            wo_ref[dy, :, 0:128] = wx_recv[dy * depth:(dy + 1) * depth, :]
            at = 3 * depth + dy * depth // 4
            tail = wx_recv[at:at + depth // 4, :]
            for k in range(4):
                wo_ref[dy, k * depth // 4:(k + 1) * depth // 4, 128:half] = tail[:, 32 * k:32 * k + 32]

    def exchange(phase, send_edges, meanwhile):
        pack_stats(stat_ref, stat_send.at[phase], height * width, matrices)
        if phase == 0:
            pl.semaphore_wait(barrier, n)
        for copy in stat_copies(phase):
            copy.start()
        send_edges()
        gathered[phase, 0] = stat_send[phase]
        if phase == 0:
            for copy in loads[0]:
                copy.wait()
        fill_sides(main_ref.at[phase], rest_ref.at[phase], side_ref)
        meanwhile()
        for copy in stat_copies(phase):
            copy.wait()
        factors = group_factors(gathered.at[phase], gains[phase:phase + 1], height * width, matrices)
        wait_edges(phase)
        return factors

    def activate(mean, scale):
        half_scale = scale * 0.5

        def act(t, valid=None):
            z = (t - mean) * half_scale
            z = z + z * jnp.tanh(z)
            return z if valid is None else jnp.where(valid, z, 0.0)

        return act

    def filler(phase, source, mean, scale):
        act = activate(mean, scale)

        def border_act(v, valid):
            v = v.astype(jnp.float32)
            if phase == 0:
                t = add_cloud(v[:, :channels], v[:, 384:512], cloud_ref)
            else:
                t = v[:, :channels] + embed_ref[...]
            return act(t, valid)

        halo_ref[0, 1:height + 1, :] = border_act(col_recv[phase, 0], valid_left)
        halo_ref[1, 1:height + 1, :] = border_act(col_recv[phase, 1], valid_right)

        def fill(i, q_ref):
            at = pl.ds(pl.multiple_of(i * ROWS, ROWS), 16)
            count = ROWS + 2
            fill_columns(
                q_ref, 0, act(source(pl.multiple_of(i * cells - width, width), count * width)),
                halo_ref[0, at, :][0:count], halo_ref[1, at, :][0:count], count, width,
            )

        def border(k, q_ref):
            valid = valid_down if k else valid_up
            lcol = border_act(corner_recv[phase, k, 0], valid_left & valid)[15:16, :]
            rcol = border_act(corner_recv[phase, k, 1], valid_right & valid)[0:1, :]
            fill_columns(
                q_ref, (ROWS + 1) * width if k else 0, border_act(row_recv[phase, k], valid), lcol, rcol, 1, width,
            )

        def fill_first(q_ref):
            count = ROWS + 1
            fill_columns(
                q_ref, width, act(source(0, count * width)),
                halo_ref[0, 1:count + 1, :], halo_ref[1, 1:count + 1, :], count, width,
            )
            border(0, q_ref)

        return fill, fill_first, border

    stat_ref[...] = jnp.zeros_like(stat_ref)
    ones = lax.broadcasted_iota(jnp.int32, (ROWS, ROWS * 128), 1) // 128
    ones = (ones == lax.broadcasted_iota(jnp.int32, (ROWS, ROWS * 128), 0)).astype(jnp.float32).astype(jnp.bfloat16)

    def spread_mask(i, carry):
        m = mask_in[pl.ds(pl.multiple_of(i * ROWS, ROWS), ROWS), :].astype(jnp.float32).astype(jnp.bfloat16)
        wide = lax.dot_general(m, ones, (((0,), (0,)), ((), ())), preferred_element_type=jnp.float32)
        for r in range(ROWS):
            at = pl.ds(pl.multiple_of(i * cells + r * width, width), width)
            mask_ref[at, :] = wide[:, r * 128:(r + 1) * 128].astype(jnp.bfloat16)
        return carry

    lax.fori_loop(0, chunks, spread_mask, 0)
    for copy in small:
        copy.wait()
    angles = lax.broadcasted_iota(jnp.int32, (16, half), 1).astype(jnp.float32)
    angles = step_in[0].astype(jnp.float32) * jnp.exp(-math.log(10000.0) * angles / half)
    embed = sum(
        jnp.dot(wave(angles).astype(jnp.bfloat16), time_ref[k * half:(k + 1) * half, :], preferred_element_type=jnp.float32)
        for k, wave in enumerate((jnp.cos, jnp.sin))
    )[0:1, :]
    embed_ref[...] = embed / (1.0 + jnp.exp(-embed))
    zero = zero_ref[...].astype(jnp.float32)
    line = lax.broadcasted_iota(jnp.int32, (channels, 1), 0)

    def place(start, stop, count, repeat):
        lane = lax.broadcasted_iota(jnp.int32, (channels, count), 1)
        shift = (stop + half) % channels
        unit = jnp.where(line == lane + shift, 1.0, 0.0)
        part = jnp.where(me_s == 0, zero[:, stop:stop + count], unit).astype(jnp.float32)
        part = jnp.concatenate([part] * repeat, axis=1) if repeat > 1 else part
        mix_ref[:, start:start + count * repeat] = part.astype(jnp.bfloat16)

    mix_ref[:, 128:256] = jnp.zeros((channels, 128), jnp.bfloat16)
    place(0, 0, half, 1)
    place(256, half, 128, 1)
    place(384, half + 128, 32, 4)

    def first_stats(i, carry):
        load_x(i).wait()
        at = pl.ds(pl.multiple_of(i * cells, cells), cells)
        x, m = x_ref[at, :].astype(jnp.float32), mask_ref[at, :].astype(jnp.float32)
        store_columns(x, width, stage_ref, 0, i)
        store_columns(m, width, stage_ref, 384, i)
        merge_stats(stat_ref, add_cloud(x, m, cloud_ref), i)
        return carry

    lax.fori_loop(0, chunks, first_stats, 0)
    pack_columns(0, 0, height)
    for side, start in ((0, 0), (1, last_row)):
        row_send[0, side, :, 0:channels] = x_ref[start:start + width, :]
        row_send[0, side, :, 384:512] = mask_ref[start:start + width, :]

    def prepare():
        share_weights()
        share_inputs()

    factors = exchange(0, lambda: start_edges(0, ("row", 0), ("row", 1), ("col", 0), ("col", 1)), prepare)
    stat_ref[...] = jnp.zeros_like(stat_ref)

    def first_step(i, q_ref):
        t = conv_chunk(q_ref, main_ref.at[0], rest_ref.at[0], side_ref, width) + embed_ref[...]
        mid_ref[pl.ds(pl.multiple_of(i * cells, cells), cells), :] = t

    def observe(i):
        t = mid_ref[pl.ds(pl.multiple_of(i * cells, cells), cells), :]
        store_columns(t, width, stage_ref, 0, i)
        merge_stats(stat_ref, t, i)

    def send_row(side, start):
        row_send[1, side, :, 0:channels] = (mid_ref[start:start + width, :] - embed_ref[...]).astype(jnp.bfloat16)
        start_edges(1, ("row", side))

    def send_early():
        pack_columns(1, 0, early)
        start_edges(1, ("col", 0))

    fill, fill_first, border = filler(0, load, *factors)
    fill_first(qa_ref)
    fill(1, qb_ref)
    first_step(0, qa_ref)
    send_row(0, 0)
    share_middle(0)
    weight_ship().wait()
    for copy in column_ships():
        copy.start()

    def first_pair(k, carry):
        for i, here, there in ((2 * k + 1, qb_ref, qa_ref), (2 * k + 2, qa_ref, qb_ref)):
            observe(i - 1)
            fill(i + 1, there)
            first_step(i, here)

        @pl.when(2 * k + 2 == SHARED)
        def _():
            for j in range(1, SHARED):
                share_middle(j)
            share_line()

        return carry

    lax.fori_loop(0, chunks // 2 - 1, first_pair, 0)
    send_early()
    border(1, qb_ref)
    observe(chunks - 2)
    first_step(chunks - 1, qb_ref)
    observe(chunks - 1)

    def send_late():
        pack_columns(1, early, 16)
        start_edges(1, ("col", 1))
        send_row(1, last_row)

    def pass_weights():
        for copy in column_ships():
            copy.wait()
        for copy in core_ships():
            copy.start()

    factors = exchange(1, send_late, pass_weights)
    share_factors(*factors)
    def store_keep(i):
        at = pl.ds(pl.multiple_of(i * cells, cells), cells)
        return pltpu.make_async_copy(keep_ref.at[at], keep_hbm.at[at], keep_sem.at[i])

    def second_step(i, q_ref):
        at = pl.ds(pl.multiple_of(i * cells, cells), cells)
        t = load(pl.multiple_of(i * cells, cells), cells)
        skip = (t + conv_chunk(q_ref, main_ref.at[1], rest_ref.at[1], side_ref, width)).astype(jnp.bfloat16)
        y = jnp.dot(skip, mix_ref[...], preferred_element_type=jnp.float32)
        pack_out(i, y)
        swap(i).start()
        keep_ref[at, :] = y[:, :half].astype(jnp.bfloat16)
        store_keep(i).start()

    fill, fill_first, border = filler(1, lambda s, c: mid_ref[pl.ds(s, c), :], *factors)
    fill(SHARED, qa_ref)

    def second_pair(k, carry):
        for i, here, there in ((SHARED + 2 * k, qa_ref, qb_ref), (SHARED + 2 * k + 1, qb_ref, qa_ref)):
            fill(i + 1, there)
            second_step(i, here)
        return carry

    lax.fori_loop(0, (chunks - SHARED) // 2 - 1, second_pair, 0)
    fill(chunks - 1, qb_ref)
    border(1, qb_ref)
    second_step(chunks - 2, qa_ref)
    gather_shared()
    act = activate(fac_recv[0:1, 0:channels], fac_recv[1:2, 0:channels])

    def unpack(v):
        return v.astype(jnp.float32)[:, :channels]

    edge_ref[0] = act(unpack(cols_recv[0]), valid_left)
    edge_ref[1] = act(unpack(cols_recv[1]), valid_right)
    lcol = act(unpack(ends_recv[0]), valid_up & valid_left)[15:16, :]
    rcol = act(unpack(ends_recv[1]), valid_up & valid_right)[0:1, :]
    fill_columns(q2_ref, 0, act(unpack(top_recv[...]), valid_up), lcol, rcol, 1, width)
    fill_columns(
        q2_ref, (shared + 1) * width, act(unpack(line_recv[...])),
        edge_ref[0, shared:shared + 1, :], edge_ref[1, shared:shared + 1, :], 1, width,
    )

    for i in range(SHARED):
        tail = mid_recv[i, 2 * cells:, :].astype(jnp.float32)
        tail = jnp.concatenate([tail[:, 0:64], tail[:, 64:128]], axis=0)
        v = [mid_recv[i, k * cells:(k + 1) * cells, :].astype(jnp.float32) for k in range(2)]
        at = slice(i * ROWS, (i + 1) * ROWS)
        fill_columns(
            q2_ref, i * cells + width, act(jnp.concatenate(v + [tail], axis=1)),
            edge_ref[0, at, :], edge_ref[1, at, :], ROWS, width,
        )
    second_step(chunks - 1, qb_ref)

    def shared_step(i, q_ref):
        at = slice(i * cells, (i + 1) * cells)
        t = base_ref[at, :]
        for dy in range(3):
            a = q_ref[dy * width:dy * width + cells, :]
            t = t + jnp.dot(a, wk_ref[dy], preferred_element_type=jnp.float32)
            a = q2_ref[i * cells + dy * width:(i + 1) * cells + dy * width, :]
            t = t + jnp.dot(a, wo_ref[dy], preferred_element_type=jnp.float32)
        keep_ref[at, :] = t.astype(jnp.bfloat16)
        store_keep(i).start()

    fill_first(qa_ref)
    for i in range(SHARED):
        here, there = (qb_ref, qa_ref) if i % 2 else (qa_ref, qb_ref)
        if i + 1 < SHARED:
            fill(i + 1, there)
        shared_step(i, here)

    def finish(i, carry):
        store_keep(i).wait()
        swap(i).wait()
        return carry

    lax.fori_loop(0, chunks, finish, 0)


def fold(y):
    quarter = y.shape[0] // 4
    lane = lax.broadcasted_iota(jnp.int32, (quarter, 128), 1)
    rest = y[0:quarter]
    for k in range(1, 4):
        rest = jnp.where(lane >= 32 * k, y[k * quarter:(k + 1) * quarter], rest)
    return rest


def merge_kernel(keep_ref, got_ref, out_hbm, out_ref, sem):
    chunks, cells = got_ref.shape[0], keep_ref.shape[0] // got_ref.shape[0]
    quarter = cells // 4

    def store(i):
        at = pl.ds(pl.multiple_of(i * cells, cells), cells)
        return pltpu.make_async_copy(out_ref.at[at], out_hbm.at[at], sem.at[i])

    def merge(i, carry):
        rest = got_ref[i, cells:, :].astype(jnp.float32)
        for k in range(4):
            got = got_ref[i, k * quarter:(k + 1) * quarter, :].astype(jnp.float32)
            got = jnp.concatenate([got, rest[:, 32 * k:32 * k + 32]], axis=1)
            at = pl.ds(pl.multiple_of(i * cells + k * quarter, quarter), quarter)
            out_ref[at, :] = (keep_ref[at, :].astype(jnp.float32) + got).astype(jnp.bfloat16)
        store(i).start()
        return carry

    lax.fori_loop(0, chunks, merge, 0)

    def finish(i, carry):
        store(i).wait()
        return carry

    lax.fori_loop(0, chunks, finish, 0)


def fill_columns(q_ref, start, act, lcol, rcol, rows, width):
    channels = act.shape[1]
    v = act.reshape(rows, width, channels)
    col = lax.broadcasted_iota(jnp.int32, (rows, 8, channels), 1)
    vl, vr = pltpu.roll(v, 1, 1), pltpu.roll(v, width - 1, 1)
    head = jnp.where(col == 0, lcol.reshape(rows, 1, channels), vl[:, :8])
    tail = jnp.where(col == 7, rcol.reshape(rows, 1, channels), vr[:, width - 8:])
    vl = jnp.concatenate([head, vl[:, 8:]], axis=1)
    vr = jnp.concatenate([vr[:, :width - 8], tail], axis=1)
    at = pl.ds(start, rows * width)
    parts = [p.reshape(rows * width, channels) for p in (vl, v, vr)]
    for k, part in enumerate(parts):
        q_ref[at, k * MAIN:(k + 1) * MAIN] = part[:, :MAIN].astype(jnp.bfloat16)
    tails = [p[:, MAIN:] for p in parts]
    q_ref[at, 3 * MAIN:] = jnp.concatenate(tails, axis=1).astype(jnp.bfloat16)


def fill_sides(main_ref, rest_ref, side_ref):
    rest = side_ref.shape[2] // 4
    blank = jnp.zeros((3 * MAIN, rest), jnp.bfloat16)
    for r in range(6):
        top, low = [], []
        for k in range(4):
            dy = r - k
            inside = 0 <= dy <= 2
            top.append(main_ref[dy, :, :, MAIN:].reshape(3 * MAIN, rest) if inside else blank)
            low.append(rest_ref[dy, :, :, MAIN:].reshape(3 * rest, rest) if inside else blank[:3 * rest])
        side_ref[r, 0:3 * MAIN, :] = jnp.concatenate(top, axis=1)
        side_ref[r, 3 * MAIN:, :] = jnp.concatenate(low, axis=1)


def conv_chunk(q_ref, main_ref, rest_ref, side_ref, width):
    cells = ROWS * width
    rest = rest_ref.shape[2]

    def rows(start, count):
        return q_ref[start * width:(start + count) * width, :]

    total = None
    for dy in range(3):
        w = jnp.concatenate(
            [main_ref[dy, :, :, 0:MAIN].reshape(3 * MAIN, MAIN), rest_ref[dy, :, :, 0:MAIN].reshape(3 * rest, MAIN)], axis=0
        )
        part = jnp.dot(rows(dy, ROWS), w, preferred_element_type=jnp.float32)
        total = part if total is None else total + part
    side = None
    for r in range(6):
        a = jnp.concatenate([rows(4 * k + r, 1) for k in range(ROWS // 4)], axis=0)
        part = jnp.dot(a, side_ref[r], preferred_element_type=jnp.float32)
        side = part if side is None else side + part
    side = jnp.concatenate(
        [side[k * width:(k + 1) * width, j * rest:(j + 1) * rest] for k in range(ROWS // 4) for j in range(4)], axis=0
    )
    return jnp.concatenate([total, side], axis=1)


def per_device(streams, mask, timestep, conv_weight, norm_gain, time_weight, cloud_vec, zero_weight):
    ny, nx = lax.axis_size("gy"), lax.axis_size("gx")
    height, width, channels = streams.shape[1:]
    cells = height * width
    half = channels // 2
    x = streams.reshape(cells, channels)
    n = ny * nx
    rest = channels - MAIN
    chunks = height // ROWS
    piece = (chunks, ROWS * width * 5 // 4, 128)
    jobs = n - 1 + 10
    shared = SHARED * ROWS
    share = pl.cdiv(9 * channels * 5 // 4, 32 * nx) * 16
    dma = pltpu.SemaphoreType.DMA
    vmem = pl.BlockSpec(memory_space=VMEM)
    hbm = pl.BlockSpec(memory_space=pltpu.HBM)
    either = pl.BlockSpec(memory_space=pl.ANY)
    f4, b2 = jnp.float32, jnp.bfloat16
    keep, got = pl.pallas_call(
        functools.partial(kernel, ny, nx, height, width),
        out_shape=(VMEM((cells, half), b2), VMEM(piece, b2)),
        in_specs=[pl.BlockSpec(memory_space=pltpu.SMEM)] + [vmem] * 3 + [hbm] * 4,
        out_specs=(either, either),
        scratch_shapes=[
            VMEM((cells + width, channels), b2), VMEM((channels, channels), b2), VMEM((channels, channels), b2),
            VMEM((2, 3, 3, MAIN, channels), b2), VMEM((2, 3, 3, rest, channels), b2),
            VMEM((6, 3 * channels, 4 * rest), b2), VMEM((1, channels), f4),
            VMEM((cells + width, 128), b2), VMEM((channels, 512), b2),
            VMEM((1, channels), f4),
            VMEM(((ROWS + 2) * width, 3 * channels), b2), VMEM(((ROWS + 2) * width, 3 * channels), b2),
            VMEM((2, height + 16, channels), f4), VMEM((cells + width, channels), f4),
            VMEM((cells, half), b2), VMEM(piece, b2),
            VMEM((8, channels), f4), VMEM((2, 2, 128), f4), VMEM((2, n, 2, 128), f4),
            VMEM((2, height, 512), f4),
            VMEM((2, 2, width, 512), b2), VMEM((2, 2, height, 512), b2),
            VMEM((2, 2, width, 512), b2), VMEM((2, 2, height, 512), b2), VMEM((2, 2, 2, 16, 512), b2),
            dma((chunks,)), dma((6,)), dma((2, jobs)), dma((2, jobs)), dma((chunks,)), dma((chunks,)), dma((chunks,)),
            VMEM(((shared + 2) * width, 3 * channels), b2), VMEM((shared * width, half), f4),
            VMEM((SHARED, ROWS * width * 5 // 2, 128), b2), VMEM((SHARED, ROWS * width * 5 // 2, 128), b2),
            VMEM((2 * nx * share, 128), b2), VMEM((2 * nx * share, 128), b2),
            VMEM((3, 3 * channels, half), b2), VMEM((3, 3 * channels, half), b2),
            VMEM((width, 384), b2), VMEM((width, 384), b2), VMEM((2, 384), f4), VMEM((2, 384), f4),
            VMEM((2, shared + 16, 384), b2), VMEM((width, 384), b2), VMEM((2, 16, 384), b2),
            VMEM((2, shared + 16, channels), f4), dma((2 * nx + SHARED + 7,)), dma((2 * nx + SHARED + 7,)),
        ],
        compiler_params=pltpu.CompilerParams(
            collective_id=0, has_side_effects=True, vmem_limit_bytes=58 << 20
        ),
        name="block",
    )(timestep, mask, cloud_vec, norm_gain, x, time_weight[0], zero_weight, conv_weight[0])
    out = pl.pallas_call(
        merge_kernel,
        out_shape=bf16(cells, half),
        in_specs=[vmem] * 2,
        out_specs=hbm,
        scratch_shapes=[VMEM((cells, half), b2), dma((chunks,))],
        compiler_params=pltpu.CompilerParams(vmem_limit_bytes=8 << 20),
        name="merge",
    )(keep, got)
    return out.reshape(height, width, half)


def solution(mesh):
    return jax.shard_map(
        per_device,
        mesh=mesh,
        in_specs=(
            P("section", "gy", "gx", None),
            P("gy", "gx"),
            P(),
            P("section", None, None, None, None, None),
            P("section", None, None),
            P("section", None, None),
            P("section", None),
            P(),
        ),
        out_specs=P("gy", "gx", "section"),
        check_vma=False,
    )
```

```python
import functools
import math

import jax
import jax.numpy as jnp
from jax import lax
from jax.experimental import pallas as pl
from jax.experimental.pallas import tpu as pltpu
from jax.sharding import PartitionSpec as P

GROUPS = 32
EPS = 1e-05
ROWS = 8
MAIN = 256
SHARED = 2
MESH = pl.DeviceIdType.MESH
VMEM = pltpu.VMEM


def bf16(*shape):
    return jax.ShapeDtypeStruct(shape, jnp.bfloat16)


def add_cloud(x, m, cloud_ref):
    channels = x.shape[1]
    m = jnp.concatenate([m] * pl.cdiv(channels, 128), axis=1)[:, :channels]
    return x + m * cloud_ref[...]


def load_inputs(x_ref, mask_ref, cloud_ref, start, count):
    x = x_ref[pl.ds(start, count), :].astype(jnp.float32)
    return add_cloud(x, mask_ref[pl.ds(start, count), :].astype(jnp.float32), cloud_ref)


def merge_stats(stat_ref, t, index):
    cells = t.shape[0]
    mean = jnp.sum(t, axis=0, keepdims=True) / cells
    diff = t - mean
    square = jnp.sum(diff * diff, axis=0, keepdims=True)
    k = jnp.asarray(index, jnp.float32)
    delta = mean - stat_ref[0:1, :]
    stat_ref[0:1, :] = stat_ref[0:1, :] + delta / (k + 1.0)
    stat_ref[1:2, :] = stat_ref[1:2, :] + square + delta * delta * (cells * k / (k + 1.0))


def store_columns(t, width, stage_ref, lane, index):
    count = t.shape[1]
    t3 = t.reshape(ROWS, width, count)
    at = pl.ds(pl.multiple_of(index * ROWS, ROWS), ROWS)
    stage_ref[0, at, lane:lane + count] = t3[:, 0, :]
    stage_ref[1, at, lane:lane + count] = t3[:, width - 1, :]


def split_rows(v):
    high = v.astype(jnp.bfloat16)
    left = v - high.astype(jnp.float32)
    mid = left.astype(jnp.bfloat16)
    low = (left - mid.astype(jnp.float32)).astype(jnp.bfloat16)
    return high, mid, low


def exact_dot(rows, matrix):
    count = rows.shape[0]
    parts = jnp.concatenate([p.astype(jnp.float32) for p in split_rows(rows)], axis=0).astype(jnp.bfloat16)
    y = jnp.dot(parts, matrix, preferred_element_type=jnp.float32)
    return y[0:count] + (y[count:2 * count] + y[2 * count:3 * count])


def group_matrices(channels):
    per = channels // GROUPS

    def member(shape, axis):
        c = lax.broadcasted_iota(jnp.int32, shape, axis)
        g = lax.broadcasted_iota(jnp.int32, shape, 1 - axis)
        return jnp.where((c >= g * per) & (c < g * per + per), 1.0, 0.0).astype(jnp.bfloat16)

    return member((channels, 128), 0), member((128, channels), 1)


def pack_stats(stat_ref, send_ref, cells, matrices):
    to_group, to_channel = matrices
    channels = stat_ref.shape[1]
    per = channels // GROUPS
    mean, square = stat_ref[0:1, :], stat_ref[1:2, :]
    total = exact_dot(jnp.broadcast_to(mean, (8, channels)), to_group)
    off = mean - exact_dot(total / per, to_channel)[0:1, :]
    square = square + cells * off * off
    squares = exact_dot(jnp.broadcast_to(square, (8, channels)), to_group)
    row = lax.broadcasted_iota(jnp.int32, (8, 128), 0)
    send_ref[...] = jnp.where(row < 1, total / per, squares)[0:2, :]


def group_factors(g_ref, gain, cells, matrices):
    n = g_ref.shape[0]
    per = gain.shape[1] // GROUPS
    values = g_ref[...]
    sums = jnp.sum(values, axis=0)
    mean = jnp.broadcast_to(sums[0:1, :] / n, (8, 128))
    off = values - mean[None, 0:2]
    total = sums[1:2, :] + float(cells * per) * jnp.sum(off * off, axis=0)[0:1, :]
    inverse = jnp.broadcast_to(lax.rsqrt(total / (float(cells) * n * per) + EPS), (8, 128))
    return exact_dot(mean, matrices[1])[0:1, :], exact_dot(inverse, matrices[1])[0:1, :] * gain


def kernel(ny, nx, height, width, step_in, mask_in, cloud_in, gain_in, x_hbm, time_hbm, zero_hbm, w_hbm, keep_hbm, got_hbm,
           x_ref, time_ref, zero_ref, main_ref, rest_ref, side_ref, embed_ref,
           mask_ref, mix_ref, cloud_ref, qa_ref, qb_ref, halo_ref, mid_ref, keep_ref, out_buf, stat_ref, stat_send, gathered,
           stage_ref, row_send, col_send, row_recv, col_recv, corner_recv, x_sem, w_sem, send, recv, keep_sem, swap_send, swap_recv,
           q2_ref, base_ref, mid_send, mid_recv, wx_send, wx_recv, wk_ref, wo_ref, line_send, line_recv, fac_send, fac_recv,
           cols_recv, top_recv, ends_recv, edge_ref, ex_send, ex_recv, fused_ref, tail_ref, late_ref, late_tail):
    me_s, me_y, me_x = lax.axis_index("section"), lax.axis_index("gy"), lax.axis_index("gx")
    n = ny * nx
    channels = x_ref.shape[1]
    half = keep_hbm.shape[1]
    cells = ROWS * width
    chunks = height // ROWS
    other = {"section": 1 - me_s}

    def near(dy, dx):
        return {"gy": lax.rem(me_y + dy + ny, ny), "gx": lax.rem(me_x + dx + nx, nx)}

    def load_x(i):
        at = pl.ds(i * cells if isinstance(i, int) else pl.multiple_of(i * cells, cells), cells)
        return pltpu.make_async_copy(x_hbm.at[at], x_ref.at[at], x_sem.at[i])

    for i in range(chunks):
        load_x(i).start()
    rest = channels - MAIN
    loads = []
    for k in range(2):
        loads.append([
            pltpu.make_async_copy(w_hbm.at[k, :, :, pl.ds(0, MAIN)], main_ref.at[k], w_sem.at[2 * k]),
            pltpu.make_async_copy(w_hbm.at[k, :, :, pl.ds(MAIN, rest)], rest_ref.at[k], w_sem.at[2 * k + 1]),
        ])
    small = [
        pltpu.make_async_copy(time_hbm, time_ref, w_sem.at[4]),
        pltpu.make_async_copy(zero_hbm, zero_ref, w_sem.at[5]),
    ]
    for copy in small + loads[1] + loads[0]:
        copy.start()
    barrier = pltpu.get_barrier_semaphore()
    for d in range(1, n):
        pl.semaphore_signal(barrier, inc=1, device_id=near(d // nx, d % nx), device_id_type=MESH)
    pl.semaphore_signal(barrier, inc=1, device_id=other, device_id_type=MESH)
    cloud_ref[...] = cloud_in[...].astype(jnp.float32)
    gains = gain_in[0].astype(jnp.float32)
    matrices = group_matrices(channels)
    load = functools.partial(load_inputs, x_ref, mask_ref, cloud_ref)

    valid_up, valid_down = me_y > 0, me_y < ny - 1
    valid_left, valid_right = me_x > 0, me_x < nx - 1
    early = height - 16
    last_row = (height - 1) * width

    def remote(src, dst, sends, receives, target):
        return pltpu.make_async_remote_copy(
            src_ref=src, dst_ref=dst, send_sem=sends, recv_sem=receives,
            device_id=target, device_id_type=MESH,
        )

    def edge_jobs(phase):
        lanes = pl.ds(0, 512 if phase == 0 else 384)
        first, last = pl.ds(0, 16), pl.ds(width - 16, 16)
        up, down = valid_up, valid_down
        left, right = valid_left, valid_right
        rows, corner = row_send.at[phase], corner_recv.at[phase]
        cols = col_send.at[phase]
        jobs = []
        for side, dy, to, back in ((0, -1, up, down), (1, 1, down, up)):
            base = 0 if side else 1
            jobs.append((("row", side), rows.at[side, :, lanes], row_recv.at[phase, 1 - side, :, lanes], (dy, 0), to, back))
            jobs.append((("row", side), rows.at[side, last, lanes], corner.at[base, 0, :, lanes], (dy, 1), to & right, back & left))
            jobs.append((("row", side), rows.at[side, first, lanes], corner.at[base, 1, :, lanes], (dy, -1), to & left, back & right))
        for part, at in enumerate((pl.ds(0, early), pl.ds(early, 16))):
            jobs.append((("col", part), cols.at[1, at, lanes], col_recv.at[phase, 0, at, lanes], (0, 1), right, left))
            jobs.append((("col", part), cols.at[0, at, lanes], col_recv.at[phase, 1, at, lanes], (0, -1), left, right))
        return [
            (kind, functools.partial(remote, src, dst, send.at[phase, k], recv.at[phase, k], near(*step)), going, coming)
            for k, (kind, src, dst, step, going, coming) in enumerate(jobs)
        ]

    def start_edges(phase, *kinds):
        for kind, copy, going, _ in edge_jobs(phase):
            if kind in kinds:
                pl.when(going)(lambda: copy().start())

    def wait_edges(phase):
        for _, copy, going, coming in edge_jobs(phase):
            pl.when(going)(lambda: copy().wait_send())
            pl.when(coming)(lambda: copy().wait_recv())

    def pack_columns(phase, start, count):
        at = slice(start, start + count)
        for side in range(2):
            if phase == 0:
                col_send[0, side, at, :] = stage_ref[side, at, :].astype(jnp.bfloat16)
            else:
                t = stage_ref[side, at, 0:channels] - embed_ref[...]
                col_send[1, side, at, 0:channels] = t.astype(jnp.bfloat16)

    def stat_copies(phase):
        order = sorted(range(1, n), key=lambda d: -min(d % nx, nx - d % nx))
        return [
            remote(stat_send.at[phase], gathered.at[phase, d], send.at[phase, 10 + d - 1], recv.at[phase, 10 + d - 1],
                   near(d // nx, d % nx))
            for d in order
        ]

    shared = SHARED * ROWS
    parity = lax.rem(me_y, 2)
    slots = 2 * nx
    share = wx_send.shape[0] // slots
    lanes = pl.ds(0, 384)

    def ship(k, src, dst, target=other):
        return remote(src, dst, ex_send.at[k], ex_recv.at[k], target)

    def slot(column, core):
        return pl.ds(pl.multiple_of((column * 2 + core) * share, 16), share)

    def weight_ship():
        at = slot(me_x, parity)
        return ship(0, wx_send.at[at], wx_recv.at[at])

    def column_ships():
        at = slot(me_x, parity)
        return [ship(d, wx_recv.at[at], wx_recv.at[at], near(0, d)) for d in range(1, nx)]

    def core_ships():
        sibling = {"gy": me_y + 1 - 2 * parity}
        return [ship(nx + d, wx_recv.at[slot(d, parity)], wx_recv.at[slot(d, parity)], sibling) for d in range(nx)]

    first_ship = 2 * nx

    def middle_ship(i):
        return ship(first_ship + i, mid_send.at[i], mid_recv.at[i])

    def line_ship():
        return ship(first_ship + SHARED, line_send, line_recv)

    def factor_ship():
        return ship(first_ship + SHARED + 1, fac_send, fac_recv)

    def border_ships():
        k = first_ship + SHARED + 2
        cols, ends = pl.ds(0, cols_recv.shape[1]), corner_recv
        return [
            (valid_left, lambda: ship(k, col_recv.at[1, 0, cols, lanes], cols_recv.at[0, :, :])),
            (valid_right, lambda: ship(k + 1, col_recv.at[1, 1, cols, lanes], cols_recv.at[1, :, :])),
            (valid_up, lambda: ship(k + 2, row_recv.at[1, 0, :, lanes], top_recv)),
            (valid_up & valid_left, lambda: ship(k + 3, ends.at[1, 0, 0, :, lanes], ends_recv.at[0])),
            (valid_up & valid_right, lambda: ship(k + 4, ends.at[1, 0, 1, :, lanes], ends_recv.at[1])),
        ]

    def pack_out(i, y):
        quarter = cells // 4
        out_buf[i, 0:cells, :] = y[:, 256:384].astype(jnp.bfloat16)
        out_buf[i, cells:cells + quarter, :] = fold(y[:, 384:512]).astype(jnp.bfloat16)

    def swap(i):
        return pltpu.make_async_remote_copy(
            src_ref=out_buf.at[i], dst_ref=got_hbm.at[i], send_sem=swap_send.at[i], recv_sem=swap_recv.at[i],
            device_id=other, device_id_type=MESH,
        )

    def share_weights():
        for copy in loads[1]:
            copy.wait()
        depth = 3 * channels
        for dy in range(3):
            w = jnp.concatenate(
                [main_ref[1, dy].reshape(3 * MAIN, channels), rest_ref[1, dy].reshape(3 * rest, channels)], axis=0
            )
            y = jnp.dot(w, mix_ref[...], preferred_element_type=jnp.float32)
            wk_ref[dy] = y[:, :half].astype(jnp.bfloat16)
            fused, tail = regroup(y)
            fused_ref[dy] = fused.astype(jnp.bfloat16)
            tail_ref[dy] = tail.astype(jnp.bfloat16)
            wx_send[dy * depth:(dy + 1) * depth, :] = y[:, 256:384].astype(jnp.bfloat16)
            at = 3 * depth + dy * depth // 4
            wx_send[at:at + depth // 4, :] = fold(y[:, 384:512]).astype(jnp.bfloat16)
        weight_ship().start()

    def share_inputs(begin, end):
        for i in range(begin, end):
            t = load(i * cells, cells).astype(jnp.bfloat16)
            y = jnp.dot(t, mix_ref[...], preferred_element_type=jnp.float32)
            base_ref[i * cells:(i + 1) * cells, :] = y[:, :half]
            pack_out(i, y)
            swap(i).start()

    def share_middle(i):
        v = mid_ref[i * cells:(i + 1) * cells, :] - embed_ref[...]
        mid_send[i, 0:cells, :] = v[:, 0:128].astype(jnp.bfloat16)
        mid_send[i, cells:2 * cells, :] = v[:, 128:256].astype(jnp.bfloat16)
        tail = jnp.concatenate([v[:cells // 2, 256:], v[cells // 2:, 256:]], axis=1)
        mid_send[i, 2 * cells:, :] = tail.astype(jnp.bfloat16)
        middle_ship(i).start()

    def share_line():
        v = mid_ref[shared * width:(shared + 1) * width, :] - embed_ref[...]
        line_send[:, 0:channels] = v.astype(jnp.bfloat16)
        line_ship().start()

    def share_factors(mean, scale):
        fac_send[0:1, 0:channels] = mean - embed_ref[...]
        fac_send[1:2, 0:channels] = scale
        factor_ship().start()
        for valid, copy in border_ships():
            pl.when(valid)(lambda: copy().start())

    def gather_shared():
        for copy in core_ships() + [middle_ship(i) for i in range(SHARED)] + [line_ship(), factor_ship()]:
            copy.wait()
        for valid, copy in border_ships():
            pl.when(valid)(lambda: copy().wait())
        depth = 3 * channels
        for dy in range(3):
            wo_ref[dy, :, 0:128] = wx_recv[dy * depth:(dy + 1) * depth, :]
            at = 3 * depth + dy * depth // 4
            tail = wx_recv[at:at + depth // 4, :]
            for k in range(4):
                wo_ref[dy, k * depth // 4:(k + 1) * depth // 4, 128:half] = tail[:, 32 * k:32 * k + 32]

    def exchange(phase, send_edges, meanwhile):
        pack_stats(stat_ref, stat_send.at[phase], height * width, matrices)
        if phase == 0:
            pl.semaphore_wait(barrier, n)
        for copy in stat_copies(phase):
            copy.start()
        send_edges()
        gathered[phase, 0] = stat_send[phase]
        if phase == 0:
            for copy in loads[0]:
                copy.wait()
            fill_sides(main_ref.at[0], rest_ref.at[0], side_ref)
        else:
            fill_tails(tail_ref, side_ref)
        meanwhile()
        for copy in stat_copies(phase):
            copy.wait()
        factors = group_factors(gathered.at[phase], gains[phase:phase + 1], height * width, matrices)
        wait_edges(phase)
        return factors

    def activate(mean, scale):
        half_scale = scale * 0.5

        def act(t, valid=None):
            z = (t - mean) * half_scale
            z = z + z * jnp.tanh(z)
            return z if valid is None else jnp.where(valid, z, 0.0)

        return act

    def filler(phase, source, mean, scale):
        act = activate(mean, scale)

        def border_act(v, valid):
            v = v.astype(jnp.float32)
            if phase == 0:
                t = add_cloud(v[:, :channels], v[:, 384:512], cloud_ref)
            else:
                t = v[:, :channels] + embed_ref[...]
            return act(t, valid)

        halo_ref[0, 1:height + 1, :] = border_act(col_recv[phase, 0], valid_left)
        halo_ref[1, 1:height + 1, :] = border_act(col_recv[phase, 1], valid_right)

        def fill(i, q_ref):
            at = pl.ds(pl.multiple_of(i * ROWS, ROWS), 16)
            count = ROWS + 2
            fill_columns(
                q_ref, 0, act(source(pl.multiple_of(i * cells - width, width), count * width)),
                halo_ref[0, at, :][0:count], halo_ref[1, at, :][0:count], count, width,
            )

        def border(k, q_ref):
            valid = valid_down if k else valid_up
            lcol = border_act(corner_recv[phase, k, 0], valid_left & valid)[15:16, :]
            rcol = border_act(corner_recv[phase, k, 1], valid_right & valid)[0:1, :]
            fill_columns(
                q_ref, (ROWS + 1) * width if k else 0, border_act(row_recv[phase, k], valid), lcol, rcol, 1, width,
            )

        def fill_first(q_ref):
            count = ROWS + 1
            fill_columns(
                q_ref, width, act(source(0, count * width)),
                halo_ref[0, 1:count + 1, :], halo_ref[1, 1:count + 1, :], count, width,
            )
            border(0, q_ref)

        return fill, fill_first, border

    stat_ref[...] = jnp.zeros_like(stat_ref)
    ones = lax.broadcasted_iota(jnp.int32, (ROWS, ROWS * 128), 1) // 128
    ones = (ones == lax.broadcasted_iota(jnp.int32, (ROWS, ROWS * 128), 0)).astype(jnp.float32).astype(jnp.bfloat16)

    def spread_mask(i, carry):
        m = mask_in[pl.ds(pl.multiple_of(i * ROWS, ROWS), ROWS), :].astype(jnp.float32).astype(jnp.bfloat16)
        wide = lax.dot_general(m, ones, (((0,), (0,)), ((), ())), preferred_element_type=jnp.float32)
        for r in range(ROWS):
            at = pl.ds(pl.multiple_of(i * cells + r * width, width), width)
            mask_ref[at, :] = wide[:, r * 128:(r + 1) * 128].astype(jnp.bfloat16)
        return carry

    lax.fori_loop(0, chunks, spread_mask, 0)
    for copy in small:
        copy.wait()
    angles = lax.broadcasted_iota(jnp.int32, (16, half), 1).astype(jnp.float32)
    angles = step_in[0].astype(jnp.float32) * jnp.exp(-math.log(10000.0) * angles / half)
    embed = sum(
        jnp.dot(wave(angles).astype(jnp.bfloat16), time_ref[k * half:(k + 1) * half, :], preferred_element_type=jnp.float32)
        for k, wave in enumerate((jnp.cos, jnp.sin))
    )[0:1, :]
    embed_ref[...] = embed / (1.0 + jnp.exp(-embed))
    zero = zero_ref[...].astype(jnp.float32)
    line = lax.broadcasted_iota(jnp.int32, (channels, 1), 0)

    def place(start, stop, count, repeat):
        lane = lax.broadcasted_iota(jnp.int32, (channels, count), 1)
        shift = (stop + half) % channels
        unit = jnp.where(line == lane + shift, 1.0, 0.0)
        part = jnp.where(me_s == 0, zero[:, stop:stop + count], unit).astype(jnp.float32)
        part = jnp.concatenate([part] * repeat, axis=1) if repeat > 1 else part
        mix_ref[:, start:start + count * repeat] = part.astype(jnp.bfloat16)

    mix_ref[:, 128:256] = jnp.zeros((channels, 128), jnp.bfloat16)
    place(0, 0, half, 1)
    place(256, half, 128, 1)
    place(384, half + 128, 32, 4)

    def first_stats(i, carry):
        load_x(i).wait()
        at = pl.ds(pl.multiple_of(i * cells, cells), cells)
        x, m = x_ref[at, :].astype(jnp.float32), mask_ref[at, :].astype(jnp.float32)
        store_columns(x, width, stage_ref, 0, i)
        store_columns(m, width, stage_ref, 384, i)
        merge_stats(stat_ref, add_cloud(x, m, cloud_ref), i)
        return carry

    lax.fori_loop(0, chunks, first_stats, 0)
    pack_columns(0, 0, height)
    for side, start in ((0, 0), (1, last_row)):
        row_send[0, side, :, 0:channels] = x_ref[start:start + width, :]
        row_send[0, side, :, 384:512] = mask_ref[start:start + width, :]

    def send_first():
        start_edges(0, ("row", 0), ("row", 1), ("col", 0), ("col", 1))
        share_inputs(0, 1)
        share_weights()
        share_inputs(1, SHARED)

    factors = exchange(0, send_first, lambda: None)
    stat_ref[...] = jnp.zeros_like(stat_ref)

    def first_step(i, q_ref):
        t = conv_chunk(q_ref, main_ref.at[0], rest_ref.at[0], side_ref, width) + embed_ref[...]
        mid_ref[pl.ds(pl.multiple_of(i * cells, cells), cells), :] = t

    def observe(i):
        t = mid_ref[pl.ds(pl.multiple_of(i * cells, cells), cells), :]
        store_columns(t, width, stage_ref, 0, i)
        merge_stats(stat_ref, t, i)

    def send_row(side, start):
        row_send[1, side, :, 0:channels] = (mid_ref[start:start + width, :] - embed_ref[...]).astype(jnp.bfloat16)
        start_edges(1, ("row", side))

    def send_early():
        pack_columns(1, 0, early)
        start_edges(1, ("col", 0))

    fill, fill_first, border = filler(0, load, *factors)
    fill_first(qa_ref)
    fill(1, qb_ref)
    first_step(0, qa_ref)
    send_row(0, 0)
    share_middle(0)

    def first_pair(k, carry):
        for i, here, there in ((2 * k + 1, qb_ref, qa_ref), (2 * k + 2, qa_ref, qb_ref)):
            observe(i - 1)
            fill(i + 1, there)
            first_step(i, here)

        @pl.when(2 * k + 2 == SHARED)
        def _():
            for j in range(1, SHARED):
                share_middle(j)
            share_line()
            weight_ship().wait()
            for copy in column_ships():
                copy.start()

        return carry

    lax.fori_loop(0, chunks // 2 - 1, first_pair, 0)
    send_early()
    border(1, qb_ref)
    observe(chunks - 2)
    first_step(chunks - 1, qb_ref)
    observe(chunks - 1)

    def send_late():
        pack_columns(1, early, 16)
        start_edges(1, ("col", 1))
        send_row(1, last_row)

    def pass_weights():
        for copy in column_ships():
            copy.wait()
        for copy in core_ships():
            copy.start()

        def late_inputs(i, carry):
            at = pl.ds(pl.multiple_of(i * cells, cells), cells)
            t = load(pl.multiple_of(i * cells, cells), cells).astype(jnp.bfloat16)
            fused, tail = regroup(jnp.dot(t, mix_ref[...], preferred_element_type=jnp.float32))
            late_ref[at, :] = fused
            late_tail[at, :] = tail
            return carry

        lax.fori_loop(SHARED, chunks, late_inputs, 0)

    factors = exchange(1, send_late, pass_weights)
    share_factors(*factors)
    def store_keep(i):
        at = pl.ds(pl.multiple_of(i * cells, cells), cells)
        return pltpu.make_async_copy(keep_ref.at[at], keep_hbm.at[at], keep_sem.at[i])

    def second_step(i, q_ref):
        at = pl.ds(pl.multiple_of(i * cells, cells), cells)
        quarter = cells // 4
        fused, tail = conv_products(q_ref, lambda dy: fused_ref[dy], side_ref, width)
        fused, tail = fused + late_ref[at, :], tail + late_tail[at, :]
        out_buf[i, 0:cells, :] = fused[:, :128].astype(jnp.bfloat16)
        out_buf[i, cells:cells + quarter, :] = jnp.concatenate(
            [tail[k * quarter:(k + 1) * quarter, 0:32] for k in range(4)], axis=1
        ).astype(jnp.bfloat16)
        swap(i).start()
        keep_ref[at, :] = jnp.concatenate([fused[:, 128:], tail[:, 32:64]], axis=1).astype(jnp.bfloat16)
        store_keep(i).start()

    fill, fill_first, border = filler(1, lambda s, c: mid_ref[pl.ds(s, c), :], *factors)
    fill(SHARED, qa_ref)

    def second_pair(k, carry):
        for i, here, there in ((SHARED + 2 * k, qa_ref, qb_ref), (SHARED + 2 * k + 1, qb_ref, qa_ref)):
            fill(i + 1, there)
            second_step(i, here)
        return carry

    lax.fori_loop(0, (chunks - SHARED) // 2 - 1, second_pair, 0)
    fill(chunks - 1, qb_ref)
    border(1, qb_ref)
    second_step(chunks - 2, qa_ref)
    gather_shared()
    act = activate(fac_recv[0:1, 0:channels], fac_recv[1:2, 0:channels])

    def unpack(v):
        return v.astype(jnp.float32)[:, :channels]

    edge_ref[0] = act(unpack(cols_recv[0]), valid_left)
    edge_ref[1] = act(unpack(cols_recv[1]), valid_right)
    lcol = act(unpack(ends_recv[0]), valid_up & valid_left)[15:16, :]
    rcol = act(unpack(ends_recv[1]), valid_up & valid_right)[0:1, :]
    fill_columns(q2_ref, 0, act(unpack(top_recv[...]), valid_up), lcol, rcol, 1, width)
    fill_columns(
        q2_ref, (shared + 1) * width, act(unpack(line_recv[...])),
        edge_ref[0, shared:shared + 1, :], edge_ref[1, shared:shared + 1, :], 1, width,
    )

    for i in range(SHARED):
        tail = mid_recv[i, 2 * cells:, :].astype(jnp.float32)
        tail = jnp.concatenate([tail[:, 0:64], tail[:, 64:128]], axis=0)
        v = [mid_recv[i, k * cells:(k + 1) * cells, :].astype(jnp.float32) for k in range(2)]
        at = slice(i * ROWS, (i + 1) * ROWS)
        fill_columns(
            q2_ref, i * cells + width, act(jnp.concatenate(v + [tail], axis=1)),
            edge_ref[0, at, :], edge_ref[1, at, :], ROWS, width,
        )
    second_step(chunks - 1, qb_ref)

    def shared_step(i, q_ref):
        at = slice(i * cells, (i + 1) * cells)
        t = base_ref[at, :]
        for dy in range(3):
            a = q_ref[dy * width:dy * width + cells, :]
            t = t + jnp.dot(a, wk_ref[dy], preferred_element_type=jnp.float32)
            a = q2_ref[i * cells + dy * width:(i + 1) * cells + dy * width, :]
            t = t + jnp.dot(a, wo_ref[dy], preferred_element_type=jnp.float32)
        keep_ref[at, :] = t.astype(jnp.bfloat16)
        store_keep(i).start()

    fill_first(qa_ref)
    for i in range(SHARED):
        here, there = (qb_ref, qa_ref) if i % 2 else (qa_ref, qb_ref)
        if i + 1 < SHARED:
            fill(i + 1, there)
        shared_step(i, here)

    def finish(i, carry):
        store_keep(i).wait()
        swap(i).wait()
        return carry

    lax.fori_loop(0, chunks, finish, 0)


def fold(y):
    quarter = y.shape[0] // 4
    lane = lax.broadcasted_iota(jnp.int32, (quarter, 128), 1)
    rest = y[0:quarter]
    for k in range(1, 4):
        rest = jnp.where(lane >= 32 * k, y[k * quarter:(k + 1) * quarter], rest)
    return rest


def merge_kernel(keep_ref, got_ref, out_hbm, out_ref, sem):
    chunks, cells = got_ref.shape[0], keep_ref.shape[0] // got_ref.shape[0]
    quarter = cells // 4

    def store(i):
        at = pl.ds(pl.multiple_of(i * cells, cells), cells)
        return pltpu.make_async_copy(out_ref.at[at], out_hbm.at[at], sem.at[i])

    def merge(i, carry):
        rest = got_ref[i, cells:, :].astype(jnp.float32)
        for k in range(4):
            got = got_ref[i, k * quarter:(k + 1) * quarter, :].astype(jnp.float32)
            got = jnp.concatenate([got, rest[:, 32 * k:32 * k + 32]], axis=1)
            at = pl.ds(pl.multiple_of(i * cells + k * quarter, quarter), quarter)
            out_ref[at, :] = (keep_ref[at, :].astype(jnp.float32) + got).astype(jnp.bfloat16)
        store(i).start()
        return carry

    lax.fori_loop(0, chunks, merge, 0)

    def finish(i, carry):
        store(i).wait()
        return carry

    lax.fori_loop(0, chunks, finish, 0)


def fill_columns(q_ref, start, act, lcol, rcol, rows, width):
    channels = act.shape[1]
    v = act.reshape(rows, width, channels)
    col = lax.broadcasted_iota(jnp.int32, (rows, 8, channels), 1)
    vl, vr = pltpu.roll(v, 1, 1), pltpu.roll(v, width - 1, 1)
    head = jnp.where(col == 0, lcol.reshape(rows, 1, channels), vl[:, :8])
    tail = jnp.where(col == 7, rcol.reshape(rows, 1, channels), vr[:, width - 8:])
    vl = jnp.concatenate([head, vl[:, 8:]], axis=1)
    vr = jnp.concatenate([vr[:, :width - 8], tail], axis=1)
    at = pl.ds(start, rows * width)
    parts = [p.reshape(rows * width, channels) for p in (vl, v, vr)]
    for k, part in enumerate(parts):
        q_ref[at, k * MAIN:(k + 1) * MAIN] = part[:, :MAIN].astype(jnp.bfloat16)
    tails = [p[:, MAIN:] for p in parts]
    q_ref[at, 3 * MAIN:] = jnp.concatenate(tails, axis=1).astype(jnp.bfloat16)


def fill_sides(main_ref, rest_ref, side_ref):
    rest = side_ref.shape[2] // 4
    blank = jnp.zeros((3 * MAIN, rest), jnp.bfloat16)
    for r in range(6):
        top, low = [], []
        for k in range(4):
            dy = r - k
            inside = 0 <= dy <= 2
            top.append(main_ref[dy, :, :, MAIN:].reshape(3 * MAIN, rest) if inside else blank)
            low.append(rest_ref[dy, :, :, MAIN:].reshape(3 * rest, rest) if inside else blank[:3 * rest])
        side_ref[r, 0:3 * MAIN, :] = jnp.concatenate(top, axis=1)
        side_ref[r, 3 * MAIN:, :] = jnp.concatenate(low, axis=1)


def fill_tails(tail_ref, side_ref):
    blank = jnp.zeros(tail_ref.shape[1:], jnp.bfloat16)
    for r in range(6):
        side_ref[r] = jnp.concatenate([tail_ref[r - k] if 0 <= r - k <= 2 else blank for k in range(4)], axis=1)


def regroup(y):
    return jnp.concatenate([y[:, 256:384], y[:, 0:128]], axis=1), jnp.concatenate([y[:, 384:416], y[:, 128:160]], axis=1)


def conv_products(q_ref, weights, side_ref, width):
    cells = ROWS * width
    rest = side_ref.shape[2] // 4

    def rows(start, count):
        return q_ref[start * width:(start + count) * width, :]

    total = None
    for dy in range(3):
        part = jnp.dot(rows(dy, ROWS), weights(dy), preferred_element_type=jnp.float32)
        total = part if total is None else total + part
    side = None
    for r in range(6):
        a = jnp.concatenate([rows(4 * k + r, 1) for k in range(ROWS // 4)], axis=0)
        part = jnp.dot(a, side_ref[r], preferred_element_type=jnp.float32)
        side = part if side is None else side + part
    side = jnp.concatenate(
        [side[k * width:(k + 1) * width, j * rest:(j + 1) * rest] for k in range(ROWS // 4) for j in range(4)], axis=0
    )
    return total, side


def conv_chunk(q_ref, main_ref, rest_ref, side_ref, width):
    rest = rest_ref.shape[2]

    def weights(dy):
        return jnp.concatenate(
            [main_ref[dy, :, :, 0:MAIN].reshape(3 * MAIN, MAIN), rest_ref[dy, :, :, 0:MAIN].reshape(3 * rest, MAIN)], axis=0
        )

    return jnp.concatenate(conv_products(q_ref, weights, side_ref, width), axis=1)


def per_device(streams, mask, timestep, conv_weight, norm_gain, time_weight, cloud_vec, zero_weight):
    ny, nx = lax.axis_size("gy"), lax.axis_size("gx")
    height, width, channels = streams.shape[1:]
    cells = height * width
    half = channels // 2
    x = streams.reshape(cells, channels)
    n = ny * nx
    rest = channels - MAIN
    chunks = height // ROWS
    piece = (chunks, ROWS * width * 5 // 4, 128)
    jobs = n - 1 + 10
    shared = SHARED * ROWS
    share = pl.cdiv(9 * channels * 5 // 4, 32 * nx) * 16
    dma = pltpu.SemaphoreType.DMA
    vmem = pl.BlockSpec(memory_space=VMEM)
    hbm = pl.BlockSpec(memory_space=pltpu.HBM)
    either = pl.BlockSpec(memory_space=pl.ANY)
    f4, b2 = jnp.float32, jnp.bfloat16
    keep, got = pl.pallas_call(
        functools.partial(kernel, ny, nx, height, width),
        out_shape=(VMEM((cells, half), b2), VMEM(piece, b2)),
        in_specs=[pl.BlockSpec(memory_space=pltpu.SMEM)] + [vmem] * 3 + [hbm] * 4,
        out_specs=(either, either),
        scratch_shapes=[
            VMEM((cells + width, channels), b2), VMEM((channels, channels), b2), VMEM((channels, channels), b2),
            VMEM((2, 3, 3, MAIN, channels), b2), VMEM((2, 3, 3, rest, channels), b2),
            VMEM((6, 3 * channels, 4 * rest), b2), VMEM((1, channels), f4),
            VMEM((cells + width, 128), b2), VMEM((channels, 512), b2),
            VMEM((1, channels), f4),
            VMEM(((ROWS + 2) * width, 3 * channels), b2), VMEM(((ROWS + 2) * width, 3 * channels), b2),
            VMEM((2, height + 16, channels), f4), VMEM((cells + width, channels), f4),
            VMEM((cells, half), b2), VMEM(piece, b2),
            VMEM((8, channels), f4), VMEM((2, 2, 128), f4), VMEM((2, n, 2, 128), f4),
            VMEM((2, height, 512), f4),
            VMEM((2, 2, width, 512), b2), VMEM((2, 2, height, 512), b2),
            VMEM((2, 2, width, 512), b2), VMEM((2, 2, height, 512), b2), VMEM((2, 2, 2, 16, 512), b2),
            dma((chunks,)), dma((6,)), dma((2, jobs)), dma((2, jobs)), dma((chunks,)), dma((chunks,)), dma((chunks,)),
            VMEM(((shared + 2) * width, 3 * channels), b2), VMEM((shared * width, half), f4),
            VMEM((SHARED, ROWS * width * 5 // 2, 128), b2), VMEM((SHARED, ROWS * width * 5 // 2, 128), b2),
            VMEM((2 * nx * share, 128), b2), VMEM((2 * nx * share, 128), b2),
            VMEM((3, 3 * channels, half), b2), VMEM((3, 3 * channels, half), b2),
            VMEM((width, 384), b2), VMEM((width, 384), b2), VMEM((2, 384), f4), VMEM((2, 384), f4),
            VMEM((2, shared + 16, 384), b2), VMEM((width, 384), b2), VMEM((2, 16, 384), b2),
            VMEM((2, shared + 16, channels), f4), dma((2 * nx + SHARED + 7,)), dma((2 * nx + SHARED + 7,)),
            VMEM((3, 3 * channels, 256), b2), VMEM((3, 3 * channels, 64), b2),
            VMEM((cells, 256), f4), VMEM((cells, 64), f4),
        ],
        compiler_params=pltpu.CompilerParams(
            collective_id=0, has_side_effects=True, vmem_limit_bytes=58 << 20
        ),
        name="block",
    )(timestep, mask, cloud_vec, norm_gain, x, time_weight[0], zero_weight, conv_weight[0])
    out = pl.pallas_call(
        merge_kernel,
        out_shape=bf16(cells, half),
        in_specs=[vmem] * 2,
        out_specs=hbm,
        scratch_shapes=[VMEM((cells, half), b2), dma((chunks,))],
        compiler_params=pltpu.CompilerParams(vmem_limit_bytes=8 << 20),
        name="merge",
    )(keep, got)
    return out.reshape(height, width, half)


def solution(mesh):
    return jax.shard_map(
        per_device,
        mesh=mesh,
        in_specs=(
            P("section", "gy", "gx", None),
            P("gy", "gx"),
            P(),
            P("section", None, None, None, None, None),
            P("section", None, None),
            P("section", None, None),
            P("section", None),
            P(),
        ),
        out_specs=P("gy", "gx", "section"),
        check_vma=False,
    )
```

```python
import functools
import math

import jax
import jax.numpy as jnp
from jax import lax
from jax.experimental import pallas as pl
from jax.experimental.pallas import tpu as pltpu
from jax.sharding import PartitionSpec as P

GROUPS = 32
EPS = 1e-05
ROWS = 8
MAIN = 256
SHARED = 2
MESH = pl.DeviceIdType.MESH
VMEM = pltpu.VMEM


def bf16(*shape):
    return jax.ShapeDtypeStruct(shape, jnp.bfloat16)


def add_cloud(x, m, cloud_ref):
    channels = x.shape[1]
    m = jnp.concatenate([m] * pl.cdiv(channels, 128), axis=1)[:, :channels]
    return x + m * cloud_ref[...]


def load_inputs(x_ref, mask_ref, cloud_ref, start, count):
    x = x_ref[pl.ds(start, count), :].astype(jnp.float32)
    return add_cloud(x, mask_ref[pl.ds(start, count), :].astype(jnp.float32), cloud_ref)


def merge_stats(stat_ref, t, index):
    cells = t.shape[0]
    mean = jnp.sum(t, axis=0, keepdims=True) / cells
    diff = t - mean
    square = jnp.sum(diff * diff, axis=0, keepdims=True)
    k = jnp.asarray(index, jnp.float32)
    delta = mean - stat_ref[0:1, :]
    stat_ref[0:1, :] = stat_ref[0:1, :] + delta / (k + 1.0)
    stat_ref[1:2, :] = stat_ref[1:2, :] + square + delta * delta * (cells * k / (k + 1.0))


def store_columns(t, width, stage_ref, lane, index):
    count = t.shape[1]
    t3 = t.reshape(ROWS, width, count)
    at = pl.ds(pl.multiple_of(index * ROWS, ROWS), ROWS)
    stage_ref[0, at, lane:lane + count] = t3[:, 0, :]
    stage_ref[1, at, lane:lane + count] = t3[:, width - 1, :]


def split_rows(v):
    high = v.astype(jnp.bfloat16)
    left = v - high.astype(jnp.float32)
    mid = left.astype(jnp.bfloat16)
    low = (left - mid.astype(jnp.float32)).astype(jnp.bfloat16)
    return high, mid, low


def exact_dot(rows, matrix):
    count = rows.shape[0]
    parts = jnp.concatenate([p.astype(jnp.float32) for p in split_rows(rows)], axis=0).astype(jnp.bfloat16)
    y = jnp.dot(parts, matrix, preferred_element_type=jnp.float32)
    return y[0:count] + (y[count:2 * count] + y[2 * count:3 * count])


def group_matrices(channels):
    per = channels // GROUPS

    def member(shape, axis):
        c = lax.broadcasted_iota(jnp.int32, shape, axis)
        g = lax.broadcasted_iota(jnp.int32, shape, 1 - axis)
        return jnp.where((c >= g * per) & (c < g * per + per), 1.0, 0.0).astype(jnp.bfloat16)

    return member((channels, 128), 0), member((128, channels), 1)


def pack_stats(stat_ref, send_ref, cells, matrices):
    to_group, to_channel = matrices
    channels = stat_ref.shape[1]
    per = channels // GROUPS
    mean, square = stat_ref[0:1, :], stat_ref[1:2, :]
    total = exact_dot(jnp.broadcast_to(mean, (8, channels)), to_group)
    off = mean - exact_dot(total / per, to_channel)[0:1, :]
    square = square + cells * off * off
    squares = exact_dot(jnp.broadcast_to(square, (8, channels)), to_group)
    row = lax.broadcasted_iota(jnp.int32, (8, 128), 0)
    send_ref[...] = jnp.where(row < 1, total / per, squares)[0:2, :]


def group_factors(g_ref, gain, cells, matrices):
    n = g_ref.shape[0]
    per = gain.shape[1] // GROUPS
    values = g_ref[...]
    sums = jnp.sum(values, axis=0)
    mean = jnp.broadcast_to(sums[0:1, :] / n, (8, 128))
    off = values - mean[None, 0:2]
    total = sums[1:2, :] + float(cells * per) * jnp.sum(off * off, axis=0)[0:1, :]
    inverse = jnp.broadcast_to(lax.rsqrt(total / (float(cells) * n * per) + EPS), (8, 128))
    return exact_dot(mean, matrices[1])[0:1, :], exact_dot(inverse, matrices[1])[0:1, :] * gain


def kernel(ny, nx, height, width, step_in, mask_in, cloud_in, gain_in, x_hbm, time_hbm, zero_hbm, w_hbm, keep_hbm, got_hbm,
           x_ref, time_ref, zero_ref, main_ref, rest_ref, side_ref, embed_ref,
           mask_ref, mix_ref, cloud_ref, qa_ref, qb_ref, halo_ref, mid_ref, keep_ref, out_buf, stat_ref, stat_send, gathered,
           stage_ref, row_send, col_send, row_recv, col_recv, corner_recv, x_sem, w_sem, send, recv, keep_sem, swap_send, swap_recv,
           q2_ref, base_ref, mid_send, mid_recv, wx_send, wx_recv, wk_ref, wo_ref, line_send, line_recv, fac_send, fac_recv,
           cols_recv, top_recv, ends_recv, edge_ref, ex_send, ex_recv, fused_ref, tail_ref, late_ref, late_tail):
    me_s, me_y, me_x = lax.axis_index("section"), lax.axis_index("gy"), lax.axis_index("gx")
    n = ny * nx
    channels = x_ref.shape[1]
    half = keep_hbm.shape[1]
    cells = ROWS * width
    chunks = height // ROWS
    other = {"section": 1 - me_s}

    def near(dy, dx):
        return {"gy": lax.rem(me_y + dy + ny, ny), "gx": lax.rem(me_x + dx + nx, nx)}

    def load_x(i):
        at = pl.ds(i * cells if isinstance(i, int) else pl.multiple_of(i * cells, cells), cells)
        return pltpu.make_async_copy(x_hbm.at[at], x_ref.at[at], x_sem.at[i])

    for i in range(chunks):
        load_x(i).start()
    rest = channels - MAIN
    loads = []
    for k in range(2):
        loads.append([
            pltpu.make_async_copy(w_hbm.at[k, :, :, pl.ds(0, MAIN)], main_ref.at[k], w_sem.at[2 * k]),
            pltpu.make_async_copy(w_hbm.at[k, :, :, pl.ds(MAIN, rest)], rest_ref.at[k], w_sem.at[2 * k + 1]),
        ])
    small = [
        pltpu.make_async_copy(time_hbm, time_ref, w_sem.at[4]),
        pltpu.make_async_copy(zero_hbm, zero_ref, w_sem.at[5]),
    ]
    for copy in small + loads[1] + loads[0]:
        copy.start()
    barrier = pltpu.get_barrier_semaphore()
    for d in range(1, n):
        pl.semaphore_signal(barrier, inc=1, device_id=near(d // nx, d % nx), device_id_type=MESH)
    pl.semaphore_signal(barrier, inc=1, device_id=other, device_id_type=MESH)
    cloud_ref[...] = cloud_in[...].astype(jnp.float32)
    gains = gain_in[0].astype(jnp.float32)
    matrices = group_matrices(channels)
    load = functools.partial(load_inputs, x_ref, mask_ref, cloud_ref)

    valid_up, valid_down = me_y > 0, me_y < ny - 1
    valid_left, valid_right = me_x > 0, me_x < nx - 1
    early = height - 16
    last_row = (height - 1) * width

    def remote(src, dst, sends, receives, target):
        return pltpu.make_async_remote_copy(
            src_ref=src, dst_ref=dst, send_sem=sends, recv_sem=receives,
            device_id=target, device_id_type=MESH,
        )

    def edge_jobs(phase):
        lanes = pl.ds(0, 512 if phase == 0 else 384)
        first, last = pl.ds(0, 16), pl.ds(width - 16, 16)
        up, down = valid_up, valid_down
        left, right = valid_left, valid_right
        rows, corner = row_send.at[phase], corner_recv.at[phase]
        cols = col_send.at[phase]
        jobs = []
        for side, dy, to, back in ((0, -1, up, down), (1, 1, down, up)):
            base = 0 if side else 1
            jobs.append((("row", side), rows.at[side, :, lanes], row_recv.at[phase, 1 - side, :, lanes], (dy, 0), to, back))
            jobs.append((("row", side), rows.at[side, last, lanes], corner.at[base, 0, :, lanes], (dy, 1), to & right, back & left))
            jobs.append((("row", side), rows.at[side, first, lanes], corner.at[base, 1, :, lanes], (dy, -1), to & left, back & right))
        for part, at in enumerate((pl.ds(0, early), pl.ds(early, 16))):
            jobs.append((("col", part), cols.at[1, at, lanes], col_recv.at[phase, 0, at, lanes], (0, 1), right, left))
            jobs.append((("col", part), cols.at[0, at, lanes], col_recv.at[phase, 1, at, lanes], (0, -1), left, right))
        return [
            (kind, functools.partial(remote, src, dst, send.at[phase, k], recv.at[phase, k], near(*step)), going, coming)
            for k, (kind, src, dst, step, going, coming) in enumerate(jobs)
        ]

    def start_edges(phase, *kinds):
        for kind, copy, going, _ in edge_jobs(phase):
            if kind in kinds:
                pl.when(going)(lambda: copy().start())

    def wait_edges(phase):
        for _, copy, going, coming in edge_jobs(phase):
            pl.when(going)(lambda: copy().wait_send())
            pl.when(coming)(lambda: copy().wait_recv())

    def pack_columns(phase, start, count):
        at = slice(start, start + count)
        for side in range(2):
            if phase == 0:
                col_send[0, side, at, :] = stage_ref[side, at, :].astype(jnp.bfloat16)
            else:
                t = stage_ref[side, at, 0:channels] - embed_ref[...]
                col_send[1, side, at, 0:channels] = t.astype(jnp.bfloat16)

    def stat_copies(phase):
        order = sorted(range(1, n), key=lambda d: -min(d % nx, nx - d % nx))
        return [
            remote(stat_send.at[phase], gathered.at[phase, d], send.at[phase, 10 + d - 1], recv.at[phase, 10 + d - 1],
                   near(d // nx, d % nx))
            for d in order
        ]

    shared = SHARED * ROWS
    parity = lax.rem(me_y, 2)
    slots = 2 * nx
    share = wx_send.shape[0] // slots
    lanes = pl.ds(0, 384)

    def ship(k, src, dst, target=other):
        return remote(src, dst, ex_send.at[k], ex_recv.at[k], target)

    def slot(column, core):
        return pl.ds(pl.multiple_of((column * 2 + core) * share, 16), share)

    def weight_ship():
        at = slot(me_x, parity)
        return ship(0, wx_send.at[at], wx_recv.at[at])

    def column_ships():
        at = slot(me_x, parity)
        return [ship(d, wx_recv.at[at], wx_recv.at[at], near(0, d)) for d in range(1, nx)]

    def core_ships():
        sibling = {"gy": me_y + 1 - 2 * parity}
        return [ship(nx + d, wx_recv.at[slot(d, parity)], wx_recv.at[slot(d, parity)], sibling) for d in range(nx)]

    first_ship = 2 * nx

    def middle_ship(i):
        return ship(first_ship + i, mid_send.at[i], mid_recv.at[i])

    def line_ship():
        return ship(first_ship + SHARED, line_send, line_recv)

    def factor_ship():
        return ship(first_ship + SHARED + 1, fac_send, fac_recv)

    def border_ships():
        k = first_ship + SHARED + 2
        cols, ends = pl.ds(0, cols_recv.shape[1]), corner_recv
        return [
            (valid_left, lambda: ship(k, col_recv.at[1, 0, cols, lanes], cols_recv.at[0, :, :])),
            (valid_right, lambda: ship(k + 1, col_recv.at[1, 1, cols, lanes], cols_recv.at[1, :, :])),
            (valid_up, lambda: ship(k + 2, row_recv.at[1, 0, :, lanes], top_recv)),
            (valid_up & valid_left, lambda: ship(k + 3, ends.at[1, 0, 0, :, lanes], ends_recv.at[0])),
            (valid_up & valid_right, lambda: ship(k + 4, ends.at[1, 0, 1, :, lanes], ends_recv.at[1])),
        ]

    def pack_out(i, y):
        quarter = cells // 4
        out_buf[i, 0:cells, :] = y[:, 256:384].astype(jnp.bfloat16)
        out_buf[i, cells:cells + quarter, :] = fold(y[:, 384:512]).astype(jnp.bfloat16)

    def swap(i):
        return pltpu.make_async_remote_copy(
            src_ref=out_buf.at[i], dst_ref=got_hbm.at[i], send_sem=swap_send.at[i], recv_sem=swap_recv.at[i],
            device_id=other, device_id_type=MESH,
        )

    def share_weights():
        for copy in loads[1]:
            copy.wait()
        depth = 3 * channels
        for dy in range(3):
            w = jnp.concatenate(
                [main_ref[1, dy].reshape(3 * MAIN, channels), rest_ref[1, dy].reshape(3 * rest, channels)], axis=0
            )
            y = jnp.dot(w, mix_ref[...], preferred_element_type=jnp.float32)
            wk_ref[dy] = y[:, :half].astype(jnp.bfloat16)
            fused, tail = regroup(y)
            fused_ref[dy] = fused.astype(jnp.bfloat16)
            tail_ref[dy] = tail.astype(jnp.bfloat16)
            wx_send[dy * depth:(dy + 1) * depth, :] = y[:, 256:384].astype(jnp.bfloat16)
            at = 3 * depth + dy * depth // 4
            wx_send[at:at + depth // 4, :] = fold(y[:, 384:512]).astype(jnp.bfloat16)
        weight_ship().start()

    def share_inputs(begin, end):
        for i in range(begin, end):
            t = load(i * cells, cells).astype(jnp.bfloat16)
            y = jnp.dot(t, mix_ref[...], preferred_element_type=jnp.float32)
            base_ref[i * cells:(i + 1) * cells, :] = y[:, :half]
            pack_out(i, y)
            swap(i).start()

    def share_middle(i):
        v = mid_ref[i * cells:(i + 1) * cells, :] - embed_ref[...]
        mid_send[i, 0:cells, :] = v[:, 0:128].astype(jnp.bfloat16)
        mid_send[i, cells:2 * cells, :] = v[:, 128:256].astype(jnp.bfloat16)
        tail = jnp.concatenate([v[:cells // 2, 256:], v[cells // 2:, 256:]], axis=1)
        mid_send[i, 2 * cells:, :] = tail.astype(jnp.bfloat16)
        middle_ship(i).start()

    def share_line():
        v = mid_ref[shared * width:(shared + 1) * width, :] - embed_ref[...]
        line_send[:, 0:channels] = v.astype(jnp.bfloat16)
        line_ship().start()

    def share_factors(mean, scale):
        fac_send[0:1, 0:channels] = mean - embed_ref[...]
        fac_send[1:2, 0:channels] = scale
        factor_ship().start()
        for valid, copy in border_ships():
            pl.when(valid)(lambda: copy().start())

    def gather_shared():
        for copy in core_ships() + [middle_ship(i) for i in range(SHARED)] + [line_ship(), factor_ship()]:
            copy.wait()
        for valid, copy in border_ships():
            pl.when(valid)(lambda: copy().wait())
        depth = 3 * channels
        for dy in range(3):
            wo_ref[dy, :, 0:128] = wx_recv[dy * depth:(dy + 1) * depth, :]
            at = 3 * depth + dy * depth // 4
            tail = wx_recv[at:at + depth // 4, :]
            for k in range(4):
                wo_ref[dy, k * depth // 4:(k + 1) * depth // 4, 128:half] = tail[:, 32 * k:32 * k + 32]

    def exchange(phase, send_edges, meanwhile):
        pack_stats(stat_ref, stat_send.at[phase], height * width, matrices)
        if phase == 0:
            pl.semaphore_wait(barrier, n)
        for copy in stat_copies(phase):
            copy.start()
        send_edges()
        gathered[phase, 0] = stat_send[phase]
        if phase == 0:
            for copy in loads[0]:
                copy.wait()
            fill_sides(main_ref.at[0], rest_ref.at[0], side_ref)
        else:
            fill_tails(tail_ref, side_ref)
        meanwhile()
        for copy in stat_copies(phase):
            copy.wait()
        factors = group_factors(gathered.at[phase], gains[phase:phase + 1], height * width, matrices)
        wait_edges(phase)
        return factors

    def activate(mean, scale):
        half_scale = scale * 0.5

        def act(t, valid=None):
            z = (t - mean) * half_scale
            z = z + z * jnp.tanh(z)
            return z if valid is None else jnp.where(valid, z, 0.0)

        return act

    def filler(phase, source, mean, scale):
        act = activate(mean, scale)

        def border_act(v, valid):
            v = v.astype(jnp.float32)
            if phase == 0:
                t = add_cloud(v[:, :channels], v[:, 384:512], cloud_ref)
            else:
                t = v[:, :channels] + embed_ref[...]
            return act(t, valid)

        halo_ref[0, 1:height + 1, :] = border_act(col_recv[phase, 0], valid_left)
        halo_ref[1, 1:height + 1, :] = border_act(col_recv[phase, 1], valid_right)

        def fill(i, q_ref):
            at = pl.ds(pl.multiple_of(i * ROWS, ROWS), 16)
            count = ROWS + 2
            fill_columns(
                q_ref, 0, act(source(pl.multiple_of(i * cells - width, width), count * width)),
                halo_ref[0, at, :][0:count], halo_ref[1, at, :][0:count], count, width,
            )

        def border(k, q_ref):
            valid = valid_down if k else valid_up
            lcol = border_act(corner_recv[phase, k, 0], valid_left & valid)[15:16, :]
            rcol = border_act(corner_recv[phase, k, 1], valid_right & valid)[0:1, :]
            fill_columns(
                q_ref, (ROWS + 1) * width if k else 0, border_act(row_recv[phase, k], valid), lcol, rcol, 1, width,
            )

        def fill_first(q_ref):
            count = ROWS + 1
            fill_columns(
                q_ref, width, act(source(0, count * width)),
                halo_ref[0, 1:count + 1, :], halo_ref[1, 1:count + 1, :], count, width,
            )
            border(0, q_ref)

        return fill, fill_first, border

    stat_ref[...] = jnp.zeros_like(stat_ref)
    ones = lax.broadcasted_iota(jnp.int32, (ROWS, ROWS * 128), 1) // 128
    ones = (ones == lax.broadcasted_iota(jnp.int32, (ROWS, ROWS * 128), 0)).astype(jnp.float32).astype(jnp.bfloat16)

    def spread_mask(i, carry):
        m = mask_in[pl.ds(pl.multiple_of(i * ROWS, ROWS), ROWS), :].astype(jnp.float32).astype(jnp.bfloat16)
        wide = lax.dot_general(m, ones, (((0,), (0,)), ((), ())), preferred_element_type=jnp.float32)
        for r in range(ROWS):
            at = pl.ds(pl.multiple_of(i * cells + r * width, width), width)
            mask_ref[at, :] = wide[:, r * 128:(r + 1) * 128].astype(jnp.bfloat16)
        return carry

    lax.fori_loop(0, chunks, spread_mask, 0)
    for copy in small:
        copy.wait()
    angles = lax.broadcasted_iota(jnp.int32, (16, half), 1).astype(jnp.float32)
    angles = step_in[0].astype(jnp.float32) * jnp.exp(-math.log(10000.0) * angles / half)
    embed = sum(
        jnp.dot(wave(angles).astype(jnp.bfloat16), time_ref[k * half:(k + 1) * half, :], preferred_element_type=jnp.float32)
        for k, wave in enumerate((jnp.cos, jnp.sin))
    )[0:1, :]
    embed_ref[...] = embed / (1.0 + jnp.exp(-embed))
    zero = zero_ref[...].astype(jnp.float32)
    line = lax.broadcasted_iota(jnp.int32, (channels, 1), 0)

    def place(start, stop, count, repeat):
        lane = lax.broadcasted_iota(jnp.int32, (channels, count), 1)
        shift = (stop + half) % channels
        unit = jnp.where(line == lane + shift, 1.0, 0.0)
        part = jnp.where(me_s == 0, zero[:, stop:stop + count], unit).astype(jnp.float32)
        part = jnp.concatenate([part] * repeat, axis=1) if repeat > 1 else part
        mix_ref[:, start:start + count * repeat] = part.astype(jnp.bfloat16)

    mix_ref[:, 128:256] = jnp.zeros((channels, 128), jnp.bfloat16)
    place(0, 0, half, 1)
    place(256, half, 128, 1)
    place(384, half + 128, 32, 4)

    def first_stats(i, carry):
        load_x(i).wait()
        at = pl.ds(pl.multiple_of(i * cells, cells), cells)
        x, m = x_ref[at, :].astype(jnp.float32), mask_ref[at, :].astype(jnp.float32)
        store_columns(x, width, stage_ref, 0, i)
        store_columns(m, width, stage_ref, 384, i)
        merge_stats(stat_ref, add_cloud(x, m, cloud_ref), i)
        return carry

    lax.fori_loop(0, chunks, first_stats, 0)
    pack_columns(0, 0, height)
    for side, start in ((0, 0), (1, last_row)):
        row_send[0, side, :, 0:channels] = x_ref[start:start + width, :]
        row_send[0, side, :, 384:512] = mask_ref[start:start + width, :]

    def send_first():
        start_edges(0, ("row", 0), ("row", 1), ("col", 0), ("col", 1))
        share_inputs(0, 1)
        share_weights()
        share_inputs(1, SHARED)

    factors = exchange(0, send_first, lambda: None)
    stat_ref[...] = jnp.zeros_like(stat_ref)

    def first_step(i, q_ref):
        t = conv_chunk(q_ref, main_ref.at[0], rest_ref.at[0], side_ref, width) + embed_ref[...]
        mid_ref[pl.ds(pl.multiple_of(i * cells, cells), cells), :] = t

    def observe(i):
        t = mid_ref[pl.ds(pl.multiple_of(i * cells, cells), cells), :]
        store_columns(t, width, stage_ref, 0, i)
        merge_stats(stat_ref, t, i)

    def send_row(side, start):
        row_send[1, side, :, 0:channels] = (mid_ref[start:start + width, :] - embed_ref[...]).astype(jnp.bfloat16)
        start_edges(1, ("row", side))

    def send_early():
        pack_columns(1, 0, early)
        start_edges(1, ("col", 0))

    fill, fill_first, border = filler(0, load, *factors)
    fill_first(qa_ref)
    fill(1, qb_ref)
    first_step(0, qa_ref)
    send_row(0, 0)
    share_middle(0)

    def first_pair(k, carry):
        for i, here, there in ((2 * k + 1, qb_ref, qa_ref), (2 * k + 2, qa_ref, qb_ref)):
            observe(i - 1)
            fill(i + 1, there)
            first_step(i, here)

        @pl.when(2 * k + 2 == SHARED)
        def _():
            for j in range(1, SHARED):
                share_middle(j)
            share_line()
            weight_ship().wait()
            for copy in column_ships():
                copy.start()

        return carry

    lax.fori_loop(0, chunks // 2 - 1, first_pair, 0)
    send_early()
    border(1, qb_ref)
    observe(chunks - 2)
    first_step(chunks - 1, qb_ref)
    observe(chunks - 1)

    def send_late():
        pack_columns(1, early, 16)
        start_edges(1, ("col", 1))
        send_row(1, last_row)

    def pass_weights():
        for copy in column_ships():
            copy.wait()
        for copy in core_ships():
            copy.start()

        def late_inputs(i, carry):
            at = pl.ds(pl.multiple_of(i * cells, cells), cells)
            t = load(pl.multiple_of(i * cells, cells), cells).astype(jnp.bfloat16)
            fused, tail = regroup(jnp.dot(t, mix_ref[...], preferred_element_type=jnp.float32))
            late_ref[at, :] = fused
            late_tail[at, :] = tail
            return carry

        lax.fori_loop(SHARED, chunks, late_inputs, 0)

    factors = exchange(1, send_late, pass_weights)
    share_factors(*factors)
    def store_keep(i):
        at = pl.ds(pl.multiple_of(i * cells, cells), cells)
        return pltpu.make_async_copy(keep_ref.at[at], keep_hbm.at[at], keep_sem.at[i])

    def second_step(i, q_ref):
        at = pl.ds(pl.multiple_of(i * cells, cells), cells)
        quarter = cells // 4
        fused, tail = conv_products(q_ref, lambda dy: fused_ref[dy], side_ref, width)
        fused, tail = fused + late_ref[at, :], tail + late_tail[at, :]
        out_buf[i, 0:cells, :] = fused[:, :128].astype(jnp.bfloat16)
        out_buf[i, cells:cells + quarter, :] = jnp.concatenate(
            [tail[k * quarter:(k + 1) * quarter, 0:32] for k in range(4)], axis=1
        ).astype(jnp.bfloat16)
        swap(i).start()
        keep_ref[at, :] = jnp.concatenate([fused[:, 128:], tail[:, 32:64]], axis=1).astype(jnp.bfloat16)
        store_keep(i).start()

    fill, fill_first, border = filler(1, lambda s, c: mid_ref[pl.ds(s, c), :], *factors)
    fill(SHARED, qa_ref)
    second_step(SHARED, qa_ref)
    fill(SHARED + 1, qb_ref)

    def second_pair(k, carry):
        for i, here, there in ((SHARED + 2 * k + 1, qb_ref, qa_ref), (SHARED + 2 * k + 2, qa_ref, qb_ref)):
            fill(i + 1, there)
            second_step(i, here)
        return carry

    lax.fori_loop(0, (chunks - SHARED) // 2 - 1, second_pair, 0)
    border(1, qb_ref)
    gather_shared()
    act = activate(fac_recv[0:1, 0:channels], fac_recv[1:2, 0:channels])

    def unpack(v):
        return v.astype(jnp.float32)[:, :channels]

    edge_ref[0] = act(unpack(cols_recv[0]), valid_left)
    edge_ref[1] = act(unpack(cols_recv[1]), valid_right)
    lcol = act(unpack(ends_recv[0]), valid_up & valid_left)[15:16, :]
    rcol = act(unpack(ends_recv[1]), valid_up & valid_right)[0:1, :]
    fill_columns(q2_ref, 0, act(unpack(top_recv[...]), valid_up), lcol, rcol, 1, width)
    fill_columns(
        q2_ref, (shared + 1) * width, act(unpack(line_recv[...])),
        edge_ref[0, shared:shared + 1, :], edge_ref[1, shared:shared + 1, :], 1, width,
    )

    for i in range(SHARED):
        tail = mid_recv[i, 2 * cells:, :].astype(jnp.float32)
        tail = jnp.concatenate([tail[:, 0:64], tail[:, 64:128]], axis=0)
        v = [mid_recv[i, k * cells:(k + 1) * cells, :].astype(jnp.float32) for k in range(2)]
        at = slice(i * ROWS, (i + 1) * ROWS)
        fill_columns(
            q2_ref, i * cells + width, act(jnp.concatenate(v + [tail], axis=1)),
            edge_ref[0, at, :], edge_ref[1, at, :], ROWS, width,
        )
    second_step(chunks - 1, qb_ref)

    def shared_step(i, q_ref):
        at = slice(i * cells, (i + 1) * cells)
        t = base_ref[at, :]
        for dy in range(3):
            a = q_ref[dy * width:dy * width + cells, :]
            t = t + jnp.dot(a, wk_ref[dy], preferred_element_type=jnp.float32)
            a = q2_ref[i * cells + dy * width:(i + 1) * cells + dy * width, :]
            t = t + jnp.dot(a, wo_ref[dy], preferred_element_type=jnp.float32)
        keep_ref[at, :] = t.astype(jnp.bfloat16)
        store_keep(i).start()

    fill_first(qa_ref)
    for i in range(SHARED):
        here, there = (qb_ref, qa_ref) if i % 2 else (qa_ref, qb_ref)
        if i + 1 < SHARED:
            fill(i + 1, there)
        shared_step(i, here)

    def finish(i, carry):
        store_keep(i).wait()
        swap(i).wait()
        return carry

    lax.fori_loop(0, chunks, finish, 0)


def fold(y):
    quarter = y.shape[0] // 4
    lane = lax.broadcasted_iota(jnp.int32, (quarter, 128), 1)
    rest = y[0:quarter]
    for k in range(1, 4):
        rest = jnp.where(lane >= 32 * k, y[k * quarter:(k + 1) * quarter], rest)
    return rest


def merge_kernel(keep_ref, got_ref, out_hbm, out_ref, sem):
    chunks, cells = got_ref.shape[0], keep_ref.shape[0] // got_ref.shape[0]
    quarter = cells // 4

    def store(i):
        at = pl.ds(pl.multiple_of(i * cells, cells), cells)
        return pltpu.make_async_copy(out_ref.at[at], out_hbm.at[at], sem.at[i])

    def merge(i, carry):
        rest = got_ref[i, cells:, :].astype(jnp.float32)
        for k in range(4):
            got = got_ref[i, k * quarter:(k + 1) * quarter, :].astype(jnp.float32)
            got = jnp.concatenate([got, rest[:, 32 * k:32 * k + 32]], axis=1)
            at = pl.ds(pl.multiple_of(i * cells + k * quarter, quarter), quarter)
            out_ref[at, :] = (keep_ref[at, :].astype(jnp.float32) + got).astype(jnp.bfloat16)
        store(i).start()
        return carry

    lax.fori_loop(0, chunks, merge, 0)

    def finish(i, carry):
        store(i).wait()
        return carry

    lax.fori_loop(0, chunks, finish, 0)


def fill_columns(q_ref, start, act, lcol, rcol, rows, width):
    channels = act.shape[1]
    v = act.reshape(rows, width, channels)
    col = lax.broadcasted_iota(jnp.int32, (rows, 8, channels), 1)
    vl, vr = pltpu.roll(v, 1, 1), pltpu.roll(v, width - 1, 1)
    head = jnp.where(col == 0, lcol.reshape(rows, 1, channels), vl[:, :8])
    tail = jnp.where(col == 7, rcol.reshape(rows, 1, channels), vr[:, width - 8:])
    vl = jnp.concatenate([head, vl[:, 8:]], axis=1)
    vr = jnp.concatenate([vr[:, :width - 8], tail], axis=1)
    at = pl.ds(start, rows * width)
    parts = [p.reshape(rows * width, channels) for p in (vl, v, vr)]
    for k, part in enumerate(parts):
        q_ref[at, k * MAIN:(k + 1) * MAIN] = part[:, :MAIN].astype(jnp.bfloat16)
    tails = [p[:, MAIN:] for p in parts]
    q_ref[at, 3 * MAIN:] = jnp.concatenate(tails, axis=1).astype(jnp.bfloat16)


def fill_sides(main_ref, rest_ref, side_ref):
    rest = side_ref.shape[2] // 4
    blank = jnp.zeros((3 * MAIN, rest), jnp.bfloat16)
    for r in range(6):
        top, low = [], []
        for k in range(4):
            dy = r - k
            inside = 0 <= dy <= 2
            top.append(main_ref[dy, :, :, MAIN:].reshape(3 * MAIN, rest) if inside else blank)
            low.append(rest_ref[dy, :, :, MAIN:].reshape(3 * rest, rest) if inside else blank[:3 * rest])
        side_ref[r, 0:3 * MAIN, :] = jnp.concatenate(top, axis=1)
        side_ref[r, 3 * MAIN:, :] = jnp.concatenate(low, axis=1)


def fill_tails(tail_ref, side_ref):
    blank = jnp.zeros(tail_ref.shape[1:], jnp.bfloat16)
    for r in range(6):
        side_ref[r] = jnp.concatenate([tail_ref[r - k] if 0 <= r - k <= 2 else blank for k in range(4)], axis=1)


def regroup(y):
    return jnp.concatenate([y[:, 256:384], y[:, 0:128]], axis=1), jnp.concatenate([y[:, 384:416], y[:, 128:160]], axis=1)


def conv_products(q_ref, weights, side_ref, width):
    cells = ROWS * width
    rest = side_ref.shape[2] // 4

    def rows(start, count):
        return q_ref[start * width:(start + count) * width, :]

    total = None
    for dy in range(3):
        part = jnp.dot(rows(dy, ROWS), weights(dy), preferred_element_type=jnp.float32)
        total = part if total is None else total + part
    side = None
    for r in range(6):
        a = jnp.concatenate([rows(4 * k + r, 1) for k in range(ROWS // 4)], axis=0)
        part = jnp.dot(a, side_ref[r], preferred_element_type=jnp.float32)
        side = part if side is None else side + part
    side = jnp.concatenate(
        [side[k * width:(k + 1) * width, j * rest:(j + 1) * rest] for k in range(ROWS // 4) for j in range(4)], axis=0
    )
    return total, side


def conv_chunk(q_ref, main_ref, rest_ref, side_ref, width):
    rest = rest_ref.shape[2]

    def weights(dy):
        return jnp.concatenate(
            [main_ref[dy, :, :, 0:MAIN].reshape(3 * MAIN, MAIN), rest_ref[dy, :, :, 0:MAIN].reshape(3 * rest, MAIN)], axis=0
        )

    return jnp.concatenate(conv_products(q_ref, weights, side_ref, width), axis=1)


def per_device(streams, mask, timestep, conv_weight, norm_gain, time_weight, cloud_vec, zero_weight):
    ny, nx = lax.axis_size("gy"), lax.axis_size("gx")
    height, width, channels = streams.shape[1:]
    cells = height * width
    half = channels // 2
    x = streams.reshape(cells, channels)
    n = ny * nx
    rest = channels - MAIN
    chunks = height // ROWS
    piece = (chunks, ROWS * width * 5 // 4, 128)
    jobs = n - 1 + 10
    shared = SHARED * ROWS
    share = pl.cdiv(9 * channels * 5 // 4, 32 * nx) * 16
    dma = pltpu.SemaphoreType.DMA
    vmem = pl.BlockSpec(memory_space=VMEM)
    hbm = pl.BlockSpec(memory_space=pltpu.HBM)
    either = pl.BlockSpec(memory_space=pl.ANY)
    f4, b2 = jnp.float32, jnp.bfloat16
    keep, got = pl.pallas_call(
        functools.partial(kernel, ny, nx, height, width),
        out_shape=(VMEM((cells, half), b2), VMEM(piece, b2)),
        in_specs=[pl.BlockSpec(memory_space=pltpu.SMEM)] + [vmem] * 3 + [hbm] * 4,
        out_specs=(either, either),
        scratch_shapes=[
            VMEM((cells + width, channels), b2), VMEM((channels, channels), b2), VMEM((channels, channels), b2),
            VMEM((2, 3, 3, MAIN, channels), b2), VMEM((2, 3, 3, rest, channels), b2),
            VMEM((6, 3 * channels, 4 * rest), b2), VMEM((1, channels), f4),
            VMEM((cells + width, 128), b2), VMEM((channels, 512), b2),
            VMEM((1, channels), f4),
            VMEM(((ROWS + 2) * width, 3 * channels), b2), VMEM(((ROWS + 2) * width, 3 * channels), b2),
            VMEM((2, height + 16, channels), f4), VMEM((cells + width, channels), f4),
            VMEM((cells, half), b2), VMEM(piece, b2),
            VMEM((8, channels), f4), VMEM((2, 2, 128), f4), VMEM((2, n, 2, 128), f4),
            VMEM((2, height, 512), f4),
            VMEM((2, 2, width, 512), b2), VMEM((2, 2, height, 512), b2),
            VMEM((2, 2, width, 512), b2), VMEM((2, 2, height, 512), b2), VMEM((2, 2, 2, 16, 512), b2),
            dma((chunks,)), dma((6,)), dma((2, jobs)), dma((2, jobs)), dma((chunks,)), dma((chunks,)), dma((chunks,)),
            VMEM(((shared + 2) * width, 3 * channels), b2), VMEM((shared * width, half), f4),
            VMEM((SHARED, ROWS * width * 5 // 2, 128), b2), VMEM((SHARED, ROWS * width * 5 // 2, 128), b2),
            VMEM((2 * nx * share, 128), b2), VMEM((2 * nx * share, 128), b2),
            VMEM((3, 3 * channels, half), b2), VMEM((3, 3 * channels, half), b2),
            VMEM((width, 384), b2), VMEM((width, 384), b2), VMEM((2, 384), f4), VMEM((2, 384), f4),
            VMEM((2, shared + 16, 384), b2), VMEM((width, 384), b2), VMEM((2, 16, 384), b2),
            VMEM((2, shared + 16, channels), f4), dma((2 * nx + SHARED + 7,)), dma((2 * nx + SHARED + 7,)),
            VMEM((3, 3 * channels, 256), b2), VMEM((3, 3 * channels, 64), b2),
            VMEM((cells, 256), f4), VMEM((cells, 64), f4),
        ],
        compiler_params=pltpu.CompilerParams(
            collective_id=0, has_side_effects=True, vmem_limit_bytes=58 << 20
        ),
        name="block",
    )(timestep, mask, cloud_vec, norm_gain, x, time_weight[0], zero_weight, conv_weight[0])
    out = pl.pallas_call(
        merge_kernel,
        out_shape=bf16(cells, half),
        in_specs=[vmem] * 2,
        out_specs=hbm,
        scratch_shapes=[VMEM((cells, half), b2), dma((chunks,))],
        compiler_params=pltpu.CompilerParams(vmem_limit_bytes=8 << 20),
        name="merge",
    )(keep, got)
    return out.reshape(height, width, half)


def solution(mesh):
    return jax.shard_map(
        per_device,
        mesh=mesh,
        in_specs=(
            P("section", "gy", "gx", None),
            P("gy", "gx"),
            P(),
            P("section", None, None, None, None, None),
            P("section", None, None),
            P("section", None, None),
            P("section", None),
            P(),
        ),
        out_specs=P("gy", "gx", "section"),
        check_vma=False,
    )
```
